256 devices in a mesh: dp: 32 (over z, x), tensor: 8 (over y, core).
Axes of the slice: x: 4, y: 4, z: 8, core: 2. Of those that a mesh axis runs over, the one named last changes fastest.
Arguments:
- tokens: bfloat16 [30720, 4096], P('dp'), may hold values from -70 to 70
- dense_weight: bfloat16 [4096, 14336], P('dp', 'tensor'), may hold values from -0.09375 to 0.09375
- left_factor: bfloat16 [64, 4096], P(None, 'tensor'), may hold values from -0.75 to 0.75
- right_factor: bfloat16 [64, 14336], P(None, 'tensor'), may hold values from -0.75 to 0.75
Outputs:
- dir_left: float32 [64, 4096], P('dp', 'tensor')
- dir_right: float32 [64, 14336], P('dp', 'tensor')
- loss: float32 [], replicated
The draws below stay inside these ranges and needn't reach their ends.
All inputs are finite; a program needn't handle non-finite values.
Results may differ from the reference program's by a relative error of at most 0.0009.
Values may be sent and summed in bfloat16 or wider, within the bound.
A program may use at most 128 MiB of HBM per device.

```python
import jax
import jax.numpy as jnp
from jax import lax

D = 4096
F = 14336
NB = 64
SI = 64
SO = 224
MID = 4096
TOK_DEV = 960
TOKENS = 30720
N_DP = 32


def draw_tokens(key, part):
    key_base, key_rows, key_cols = jax.random.split(key, 3)
    positions = jnp.arange(TOKENS, dtype=jnp.float32) / TOKENS
    row_scale = 0.5 * jnp.exp(jnp.log(3.0) * positions) * jnp.exp(jnp.log(10.0) * 0.5 * jax.random.uniform(key_rows, (TOKENS,), jnp.float32))
    col_scale = jnp.exp(jnp.log(10.0) * (jax.random.uniform(key_cols, (D,), jnp.float32) - 0.5))
    base = jnp.clip(jax.random.normal(key_base, (TOKENS, D), jnp.float32), -4.0, 4.0)
    return (base * row_scale[:, None] * col_scale[None, :]).astype(jnp.bfloat16)


def shard_levels(own_key, extent, pieces, smallest, high):
    loudness, own = 1.0, jax.random.fold_in(own_key, 6)
    for position, blocks in pieces:
        steps = jnp.exp(jax.random.uniform(jax.random.fold_in(own, position), (blocks,), jnp.float32, smallest / len(pieces), high / len(pieces)))
        loudness = loudness * jnp.repeat(steps, extent[position] // blocks).reshape([-1 if axis == position else 1 for axis in range(len(extent))])
    return loudness


def noise(rng, shape, scale, reach, cuts=(), kind=jnp.bfloat16):
    entries = jax.random.normal(rng, shape, jnp.float32) * scale
    if len(cuts) > 0:
        entries = shard_levels(rng, shape, cuts, -0.22, 0.18) * entries
    return jnp.clip(entries, min=-reach, max=reach).astype(kind)


def setup_inputs(seed: int = 0) -> dict:
    key_of = jax.random.split(jax.random.key(seed), 5)
    tokens = draw_tokens(jax.random.fold_in(key_of[4], 71), 0)
    dense_weight = noise(key_of[1], (D, F), D ** -0.5, 0.09375, ((0, 32), (1, 8)))
    left_factor = noise(key_of[2], (SI, MID), SI ** -0.5, 0.75, ((1, 8),))
    right_factor = noise(key_of[3], (NB, F), NB ** -0.5, 0.75, ((1, 8),))
    return {"tokens": tokens, "dense_weight": dense_weight, "left_factor": left_factor, "right_factor": right_factor}


epsilon = 1e-06

def round_half(values):
    rounded = values.astype(jnp.bfloat16)
    rounded = lax.optimization_barrier(rounded)
    return rounded.astype(jnp.float32)

def block_terms(token_block, dense_weight, left_blocks, right_blocks):
    tok_rows = token_block.shape[0]
    features = token_block.reshape(tok_rows, NB, SI).astype(jnp.float32)
    first_mix = round_half(jnp.einsum('tik,kij->tji', features, left_blocks.astype(jnp.float32)))
    output = jnp.einsum('tji,ijo->tjo', first_mix, right_blocks.astype(jnp.float32)).reshape(tok_rows, F)
    targets = jnp.dot(token_block, dense_weight, preferred_element_type=jnp.float32)
    residual = output - targets
    slope_rows = round_half(residual / TOKENS).reshape(tok_rows, NB, SO)
    grad_right = jnp.einsum('tji,tjo->ijo', first_mix, slope_rows).reshape(NB, F)
    back_mix = round_half(jnp.einsum('tjo,ijo->tji', slope_rows, right_blocks.astype(jnp.float32)))
    grad_left = jnp.einsum('tik,tji->kij', features, back_mix).reshape(SI, MID)
    return (grad_left, grad_right, jnp.sum(residual * residual))

def reference(tokens, dense_weight, left_factor, right_factor):
    left_blocks = left_factor.reshape(SI, NB, NB)
    right_blocks = right_factor.reshape(NB, NB, SO)
    token_blocks = tokens.reshape(N_DP, TOK_DEV, D)

    def accumulate(carry, token_block):
        terms = block_terms(token_block, dense_weight, left_blocks, right_blocks)
        return ((carry[0] + terms[0], carry[1] + terms[1], carry[2] + terms[2]), None)
    start = (jnp.zeros((SI, MID), jnp.float32), jnp.zeros((NB, F), jnp.float32), jnp.zeros((), jnp.float32))
    totals, unused = lax.scan(accumulate, start, token_blocks)
    grad_left, grad_right, squares = totals
    dir_left = grad_left * lax.rsqrt(jnp.mean(grad_left * grad_left) + epsilon)
    dir_right = grad_right * lax.rsqrt(jnp.mean(grad_right * grad_right) + epsilon)
    loss = squares / (2.0 * TOKENS)
    return (dir_left, dir_right, loss)
```

```python
import jax
import jax.numpy as jnp
from jax import lax
from jax.experimental import pallas as pl
from jax.experimental.pallas import tpu as pltpu
from jax.sharding import PartitionSpec as P

MESH = pl.DeviceIdType.MESH
F = 14336
NB = 64
SI = 64
SO = 224
MID = 4096
TOKENS = 30720
EPS = 1e-06

NX, NZ, NT = 4, 8, 8
CH = 240
NC = 4
KS = 512
HC = 896
NA = 384
BK = 128
JB = 4
NM = JB * NB
GW = HC + NM + 128
BF = jnp.bfloat16
F32 = jnp.float32
NT_DIMS = (((1,), (1,)), ((), ()))
TN_DIMS = (((0,), (0,)), ((), ()))


def dot(a, b):
    return jnp.dot(a, b, preferred_element_type=F32)


def iota(shape, axis):
    return lax.broadcasted_iota(jnp.int32, shape, axis)


def kernel(x_hbm, w_hbm, l_hbm, r_hbm, gl_out, dr_out, loss_out,
           xx, wb, lall, lown, rh, rexp, rexp2, fm, fm32, acc, slope, bmt,
           gr, gl, lossv, gg, zr, s8, xr, sc, scz, sct, glr, ssem, rsem, lsem):
    d = lax.axis_index("dp")
    t = lax.axis_index("tensor")
    x, z = d % NX, d // NX
    y, core = t // 2, t % 2
    side = ((x + 1) // 2) % 2
    q = x // 2

    def dp_dev(xv, zv):
        return {"dp": zv * NX + xv, "tensor": t}

    def t_dev(tv):
        return {"dp": d, "tensor": tv}

    partner = dp_dev(x + 1 - 2 * (x % 2), z)
    ladder = dp_dev(3 - x, z)
    zdev = (dp_dev(x, (z + 1) % NZ), dp_dev(x, (z + NZ - 1) % NZ))
    ydev = (t_dev((t + 2) % NT), t_dev((t + NT - 2) % NT))
    other = t_dev(t + 1 - 2 * core)

    ids, sends = {}, []

    def rid(key):
        return ids.setdefault(key, len(ids))

    def send(src, dst, key, dev):
        copy = pltpu.make_async_remote_copy(
            src_ref=src, dst_ref=dst, send_sem=ssem.at[len(sends)], recv_sem=rsem.at[rid(key)],
            device_id=dev, device_id_type=MESH)
        copy.start()
        sends.append(copy)

    def recv(ref, key):
        pltpu.make_async_remote_copy(
            src_ref=ref, dst_ref=ref, send_sem=ssem.at[0], recv_sem=rsem.at[rid(key)],
            device_id=ladder, device_id_type=MESH).wait_recv()

    loads = [pltpu.make_async_copy(l_hbm, lall.at[t], lsem.at[0]),
             pltpu.make_async_copy(r_hbm.at[:, pl.ds(pl.multiple_of(side * HC, 128), HC)], rh, lsem.at[1])]
    own_rows = pl.ds(pl.multiple_of(z * KS + x * BK, BK), BK)
    own_w = pltpu.make_async_copy(
        w_hbm.at[:, pl.ds(pl.multiple_of(side * HC, 128), HC)], wb.at[own_rows, :], lsem.at[2])
    own_w.start()
    for c in loads:
        c.start()
    xloads = []
    for k in range(NT):
        c = pltpu.make_async_copy(x_hbm.at[:, :, pl.ds(k * KS, KS)], xx.at[0:NC, k], lsem.at[3 + k])
        c.start()
        xloads.append(c)

    barrier = pltpu.get_barrier_semaphore()
    peers = ([dp_dev((x + k) % NX, z) for k in range(1, NX)]
             + [dp_dev(x, (z + k) % NZ) for k in range(1, NZ)]
             + [t_dev((t + k) % NT) for k in range(1, NT)])
    for dev in peers:
        pl.semaphore_signal(barrier, inc=1, device_id=dev, device_id_type=MESH)
    pl.semaphore_wait(barrier, len(peers))

    def brow(zv, u):
        r = x % 2 if u == 0 else 1 - x % 2
        return pl.ds(pl.multiple_of(zv * KS + q * 256 + r * BK, BK), BK)

    def lbrow(zv, u):
        r = x % 2 if u == 0 else 1 - x % 2
        return pl.ds(pl.multiple_of(zv * KS + (1 - q) * 256 + (1 - r) * BK, BK), BK)

    def arow(zv, v):
        qq = q if v == 0 else 1 - q
        return pl.ds(pl.multiple_of(zv * KS + qq * 256, 256), 256)

    def bref(rows):
        return wb.at[rows, NA:HC]

    def aref(rows):
        return wb.at[rows, 0:NA]

    def zat(o):
        return (z + o + NZ) % NZ

    def hops(direction, first):
        return 4 if direction == (0 if first else 1) else 3

    bcol = pl.ds(pl.multiple_of(side * HC + NA, 128), HC - NA)
    acol = pl.ds(pl.multiple_of(side * HC, 128), NA)
    obcol = pl.ds(pl.multiple_of((1 - side) * HC + NA, 128), HC - NA)
    oacol = pl.ds(pl.multiple_of((1 - side) * HC, 128), NA)

    send(w_hbm.at[:, obcol], bref(own_rows), ("injb",), partner)
    for k in range(1, NT):
        send(l_hbm, lall.at[t], ("l", k), t_dev((t + k) % NT))
    for dr in range(2):
        send(w_hbm.at[:, bcol], bref(own_rows), ("b", dr, 0, 1), zdev[dr])
    send(w_hbm.at[:, bcol], bref(own_rows), ("lb", 0, 0, 0), ladder)
    send(w_hbm.at[:, oacol], aref(own_rows), ("inja",), partner)
    send(w_hbm.at[:, acol], aref(own_rows), ("la", 0), ladder)
    for c in range(NC):
        send(x_hbm.at[c, :, pl.ds(pl.multiple_of(t * KS, KS), KS)], xx.at[NC + c, t], ("xc", c), partner)

    def b_step(u, s, dirs=(0, 1)):
        for dr in dirs:
            if s > hops(dr, u == 0):
                continue
            ref = bref(brow(zat(-s if dr == 0 else s), u))
            recv(ref, ("b", dr, u, s))
            if s < hops(dr, u == 0):
                send(ref, ref, ("b", dr, u, s + 1), zdev[dr])
            send(ref, ref, ("lb", dr, u, s), ladder)

    def lb_wait(s):
        for dr in range(2):
            for u in range(2):
                if s <= hops(dr, u == 0):
                    recv(bref(lbrow(zat(-s if dr == 0 else s), u)), ("lb", dr, u, s))

    def a_step(v, s):
        for dr in range(2):
            if s > hops(dr, v == 0):
                continue
            ref = aref(arow(zat(-s if dr == 0 else s), v))
            recv(ref, ("a", dr, v, s))
            if s < hops(dr, v == 0):
                send(ref, ref, ("a", dr, v, s + 1), zdev[dr])

    def x_cross(c):
        ref = xx.at[NC + c, t]
        recv(ref, ("xc", c))
        for dr in range(2):
            send(ref, ref, ("y", dr, c), ydev[dr])
        send(ref, ref, ("sw", 0, c), other)

    def slice_at(o):
        return (t + 2 * o + NT) % NT

    def x_hop(c):
        for dr in range(2):
            ref = xx.at[NC + c, slice_at(-1 if dr == 0 else 1)]
            recv(ref, ("y", dr, c))
            if c % 2 == dr:
                send(ref, ref, ("y2", c), ydev[dr])
            send(ref, ref, ("sw", 1 + dr, c), other)

    def x_hop2(c):
        ref = xx.at[NC + c, slice_at(2)]
        recv(ref, ("y2", c))
        send(ref, ref, ("sw", 3, c), other)

    def x_swap(c):
        to = 1 - 2 * core
        for k, o in enumerate((0, -1, 1, 2)):
            recv(xx.at[NC + c, (t + to + 2 * o + NT) % NT], ("sw", k, c))

    def first_mix(m0, mc):
        rows = mc * CH

        def part(k, carry):
            a = xx[pl.ds(m0, mc), k].reshape(rows, KS)
            p = dot(a, lown[k].reshape(KS, NM))

            @pl.when(k == 0)
            def _():
                fm32[0:rows] = p

            @pl.when(k > 0)
            def _():
                fm32[0:rows] += p
            return carry
        lax.fori_loop(0, NT, part, 0)
        mixed = fm32[0:rows].astype(BF)
        fm[pl.ds(m0, mc)] = mixed.reshape(mc, CH, NM)
        acc[pl.ds(m0, mc)] = -dot(mixed, rexp[...]).reshape(mc, CH, HC)

    def targets(m_lo, m_n, mc, r_lo, r_n):
        def part(k, carry):
            m0 = m_lo + (k % m_n) * mc
            r = r_lo + k // m_n
            zv = (z + ((r + 1) // 2) * (2 * (r % 2) - 1) + NZ) % NZ
            a = xx[pl.ds(m0, mc), zv].reshape(mc * CH, KS)
            w = wb[pl.ds(pl.multiple_of(zv * KS, KS), KS), :]
            acc[pl.ds(m0, mc)] += dot(a, w).reshape(mc, CH, HC)
            return carry
        lax.fori_loop(0, m_n * r_n, part, 0)

    for c in loads:
        c.wait()
    col_block = iota((NB, HC), 1) // SO
    for j in range(JB):
        rexp[j * NB:(j + 1) * NB] = jnp.where(col_block == j, rh[...], 0).astype(BF)
    pick = (iota((NM, NB), 0) // JB == iota((NM, NB), 1)).astype(BF)
    spread = dot(pick, rh[...])
    rexp2[...] = jnp.where(iota((NM, HC), 0) % JB == iota((NM, HC), 1) // SO, spread, 0.0).astype(BF)
    for k in range(1, NT):
        recv(lall.at[(t + NT - k) % NT], ("l", k))
    first_j = 2 * JB * t + JB * side

    def expand(il, carry):
        row, col = iota((KS, NM), 0), iota((KS, NM), 1)
        choose = jnp.where((row // NB == il) & (row % NB == first_j + col // NB), 1.0, 0.0).astype(BF)
        p = dot(lall[...].reshape(KS, KS), choose)
        keep = col % NB == (row // NB) * 8 + il
        lown[:, il] = jnp.where(keep, p, 0.0).astype(BF).reshape(NT, SI, NM)
        return carry
    lax.fori_loop(0, 8, expand, 0)

    own_w.wait()

    def inj_b():
        ref = bref(brow(z, 1))
        recv(ref, ("injb",))
        for dr in range(2):
            send(ref, ref, ("b", dr, 1, 1), zdev[dr])
        send(ref, ref, ("lb", 0, 1, 0), ladder)

    def inj_a():
        ref = aref(brow(z, 1))
        recv(ref, ("inja",))
        send(ref, ref, ("la", 1), ladder)

    inj_b()
    b_step(0, 1)
    inj_a()
    for c in xloads:
        c.wait()
    first_mix(0, 2)
    b_step(1, 1)
    own_pair = aref(arow(z, 0))
    for dr in range(2):
        send(own_pair, own_pair, ("a", dr, 0, 1), zdev[dr])
    first_mix(2, 2)
    for u in range(2):
        recv(aref(lbrow(z, u)), ("la", u))
    lad_pair = aref(arow(z, 1))
    for dr in range(2):
        send(lad_pair, lad_pair, ("a", dr, 1, 1), zdev[dr])
    x_cross(0)
    b_step(0, 2)
    b_step(1, 2)
    for u in range(2):
        recv(bref(lbrow(z, u)), ("lb", 0, u, 0))
    targets(0, 2, 2, 0, 1)
    x_cross(1)
    a_step(0, 1)
    x_hop(0)
    x_cross(2)
    a_step(1, 1)
    lb_wait(1)
    b_step(0, 3)
    x_hop(1)
    targets(0, 2, 2, 1, 2)
    b_step(1, 3)
    x_cross(3)
    x_hop2(0)
    a_step(0, 2)
    x_swap(0)
    first_mix(NC, 1)
    targets(NC, 1, 1, 0, 3)
    x_hop(2)
    x_hop2(1)
    a_step(1, 2)
    x_swap(1)
    first_mix(NC + 1, 1)
    targets(NC + 1, 1, 1, 0, 3)
    lb_wait(2)
    b_step(0, 4)
    b_step(1, 4)
    targets(0, 2, 2, 3, 2)
    x_hop(3)
    a_step(0, 3)
    targets(NC, 1, 2, 3, 2)
    x_hop2(2)
    x_hop2(3)
    x_swap(2)
    x_swap(3)
    a_step(1, 3)
    first_mix(NC + 2, 2)
    targets(NC + 2, 1, 2, 0, 5)
    lb_wait(3)
    targets(0, 4, 2, 5, 2)
    a_step(0, 4)
    a_step(1, 4)
    lb_wait(4)
    targets(0, 4, 2, 7, 1)

    gr[...] = jnp.zeros_like(gr)
    gl[...] = jnp.zeros_like(gl)
    lossv[...] = jnp.zeros_like(lossv)

    def grads(p, carry):
        m0 = 2 * p
        a = acc[pl.ds(m0, 2)].reshape(2 * CH, HC)
        lossv[...] += jnp.sum((a * a).reshape(2 * CH // 8, 8, HC), axis=0)
        slope[...] = (a * (-1.0 / TOKENS)).astype(BF)
        gr[...] += lax.dot_general(fm[pl.ds(m0, 2)].reshape(2 * CH, NM), slope[...], TN_DIMS,
                                   preferred_element_type=F32)
        bmt[...] = lax.dot_general(rexp2[...], slope[...], NT_DIMS, preferred_element_type=F32).astype(BF)

        def left(k, c2):
            b = bmt[pl.ds(pl.multiple_of(k * 32, 32), 32), :]
            gl[k] += dot(b, xx[pl.ds(m0, 2), k].reshape(2 * CH, KS))
            return c2
        lax.fori_loop(0, NT, left, 0)
        return carry
    lax.fori_loop(0, 4, grads, 0)

    right = jnp.zeros((NB, HC), F32)
    for j in range(JB):
        right += jnp.where(col_block == j, gr[j * NB:(j + 1) * NB], 0.0)
    gg[:, 0:HC] = right
    row32 = iota((32, 128), 0)
    folded = []
    for k in range(NT):
        v = jnp.zeros((32, 128), F32)
        for p in range(4):
            v += jnp.where(row32 // 8 == p, gl[k, :, p * 128:(p + 1) * 128], 0.0)
        folded.append(jnp.where((row32 // 4) % 2 == 0, v, pltpu.roll(v, 64, 1)))
    gg[:, HC:HC + NM] = jnp.transpose(jnp.concatenate(folded, axis=0))[0:SI]
    gg[:, HC + NM:GW] = jnp.full((NB, 128), jnp.sum(lossv[...]), F32)

    for k in range(1, NZ):
        rows = pl.ds(pl.multiple_of(((z + k) % NZ) * 8, 8), 8)
        send(gg.at[rows], zr.at[k], ("z", k), dp_dev(x, (z + k) % NZ))
    total = gg[pl.ds(pl.multiple_of(z * 8, 8), 8), :]
    for k in range(1, NZ):
        recv(zr.at[k], ("z", k))
        total += zr[k]
    s8[...] = total
    for k in range(1, NX):
        send(s8, xr.at[k], ("x", k), dp_dev((x + k) % NX, z))
    first = jnp.where(side == 0, total, 0.0)
    second = jnp.where(side == 0, 0.0, total)
    for k in range(1, NX):
        recv(xr.at[k], ("x", k))
        from_x = (x + NX - k) % NX
        from_side = ((from_x + 1) // 2) % 2
        v = xr[k]
        first += jnp.where(from_side == 0, v, 0.0)
        second += jnp.where(from_side == 0, 0.0, v)

    def own(v):
        out = v[0:2]
        for k in range(1, NX):
            out = jnp.where(x == k, v[2 * k:2 * k + 2], out)
        return out

    glr[t, 0:2, 0:NM] = own(first[:, HC:HC + NM])
    glr[t, 0:2, NM:2 * NM] = own(second[:, HC:HC + NM])
    for k in range(1, NT):
        send(glr.at[t], glr.at[t], ("gl", k), t_dev((t + k) % NT))
    sq_right = jnp.sum(first[:, 0:HC] * first[:, 0:HC] + second[:, 0:HC] * second[:, 0:HC])
    left_a, left_b = first[:, HC:HC + NM], second[:, HC:HC + NM]
    sq_left = jnp.sum(left_a * left_a + left_b * left_b)
    loss_xz = first[0:1, HC + NM:GW] + second[0:1, HC + NM:GW]
    srow = iota((8, 128), 0)
    sc[...] = jnp.where(srow == 0, sq_right, jnp.where(srow == 1, sq_left, 0.0))
    for k in range(1, NZ):
        send(sc, scz.at[k], ("sz", k), dp_dev(x, (z + k) % NZ))
    tot = sc[...]
    for k in range(1, NZ):
        recv(scz.at[k], ("sz", k))
        tot += scz[k]
    sct[0] = jnp.where(srow == 2, jnp.broadcast_to(loss_xz, (8, 128)), tot)
    for k in range(1, NT):
        send(sct.at[0], sct.at[k], ("st", k), t_dev((t + k) % NT))
    tot = sct[0]
    for k in range(1, NT):
        recv(sct.at[k], ("st", k))
        tot += sct[k]
    scale_right = lax.rsqrt(tot[0:1, 0:1] / (NB * F) + EPS)
    scale_left = lax.rsqrt(tot[1:2, 0:1] / (SI * MID) + EPS)
    dr_out[:, 0:HC] = own(first[:, 0:HC]) * scale_right
    dr_out[:, HC:2 * HC] = own(second[:, 0:HC]) * scale_right
    loss_out[...] = jnp.broadcast_to(tot[2:3, :] / (2.0 * TOKENS), (8, 128))
    for k in range(1, NT):
        recv(glr.at[(t + NT - k) % NT], ("gl", k))
    for k in range(NT):
        gl_out[k] = glr[k, 0:2, :] * scale_left
    for copy in sends:
        copy.wait_send()


def local(tokens, dense_weight, left_factor, right_factor):
    vmem = pl.BlockSpec(memory_space=pltpu.VMEM)
    hbm = pl.BlockSpec(memory_space=pl.ANY)
    gl, dir_right, loss = pl.pallas_call(
        kernel,
        out_shape=(jax.ShapeDtypeStruct((NT, 2, 2 * NM), F32),
                   jax.ShapeDtypeStruct((2, 2 * HC), F32),
                   jax.ShapeDtypeStruct((8, 128), F32)),
        in_specs=[hbm] * 4,
        out_specs=(vmem,) * 3,
        scratch_shapes=[
            pltpu.VMEM((2 * NC, NT, CH, KS), BF),
            pltpu.VMEM((4096, HC), BF),
            pltpu.VMEM((NT, SI, KS), BF),
            pltpu.VMEM((NT, 8, SI, NM), BF),
            pltpu.VMEM((NB, HC), BF),
            pltpu.VMEM((NM, HC), BF),
            pltpu.VMEM((NM, HC), BF),
            pltpu.VMEM((2 * NC, CH, NM), BF),
            pltpu.VMEM((2 * CH, NM), F32),
            pltpu.VMEM((2 * NC, CH, HC), F32),
            pltpu.VMEM((2 * CH, HC), BF),
            pltpu.VMEM((NM, 2 * CH), BF),
            pltpu.VMEM((NM, HC), F32),
            pltpu.VMEM((NT, 32, KS), F32),
            pltpu.VMEM((8, HC), F32),
            pltpu.VMEM((NB, GW), F32),
            pltpu.VMEM((NZ, 8, GW), F32),
            pltpu.VMEM((8, GW), F32),
            pltpu.VMEM((NX, 8, GW), F32),
            pltpu.VMEM((8, 128), F32),
            pltpu.VMEM((NZ, 8, 128), F32),
            pltpu.VMEM((NT, 8, 128), F32),
            pltpu.VMEM((NT, 8, 2 * NM), F32),
            pltpu.SemaphoreType.DMA((160,)),
            pltpu.SemaphoreType.DMA((160,)),
            pltpu.SemaphoreType.DMA((16,)),
        ],
        compiler_params=pltpu.CompilerParams(
            collective_id=0, has_side_effects=True, vmem_limit_bytes=60 * 1024 * 1024),
    )(tokens.reshape(NC, CH, 4096), dense_weight, left_factor, right_factor)
    t = lax.axis_index("tensor")
    gl = gl.reshape(NT, 2, 2, NB, JB)
    gl = lax.dynamic_slice_in_dim(gl, t * 8, 8, 3)
    dir_left = gl.transpose(1, 3, 0, 2, 4).reshape(2, 512)
    return (dir_left, dir_right, loss[0, 0])


def solution(mesh):
    in_specs = (P("dp", None), P("dp", "tensor"), P(None, "tensor"), P(None, "tensor"))
    out_specs = (P("dp", "tensor"), P("dp", "tensor"), P())
    return jax.shard_map(local, mesh=mesh, in_specs=in_specs, out_specs=out_specs, check_vma=False)
```

```python
import jax
import jax.numpy as jnp
from jax import lax
from jax.experimental import pallas as pl
from jax.experimental.pallas import tpu as pltpu
from jax.sharding import PartitionSpec as P

MESH = pl.DeviceIdType.MESH
F = 14336
NB = 64
SI = 64
SO = 224
MID = 4096
TOKENS = 30720
EPS = 1e-06

NX, NZ, NT = 4, 8, 8
CH = 240
NC = 4
KS = 512
HC = 896
NA = 384
BK = 128
JB = 4
NM = JB * NB
LW = NM + 128
BF = jnp.bfloat16
F32 = jnp.float32
NT_DIMS = (((1,), (1,)), ((), ()))
TN_DIMS = (((0,), (0,)), ((), ()))
EXTRA = (2, 3)
ORDER = (
    "rex", "l", "exp", "injb", "b010", "b011", "inja", "b110", "b111", "lb0", "xc0", "b020", "b021", "lb010",
    "a010", "a011", "lb011", "xc1", "la", "b120", "b121", "o0", "y00", "y01", "f0", "b030", "b031", "lb110",
    "f1", "xc2", "y10", "y11", "lb111", "a020", "a021", "lb020", "xc3", "lb021", "a110", "a111", "e0", "o1",
    "sw0", "o2", "y21", "b130", "b131", "lb120", "e2", "y20", "lb121", "b040", "sw2", "a031", "e1", "lb030",
    "e3", "sw1", "x00", "x01", "a030", "x02", "y30", "a121", "lb031", "o3", "x03", "y31", "f2", "a120",
    "b141", "lb130", "sw3", "x10", "lb131", "x11", "x12", "a131", "a040", "x13", "o4", "lb040", "x04", "x14",
    "o5", "lb141", "a130", "x05", "x15", "a141", "o6", "x06", "x16", "o7", "x07", "x17", "f3")


def dot(a, b):
    return jnp.dot(a, b, preferred_element_type=F32)


def iota(shape, axis):
    return lax.broadcasted_iota(jnp.int32, shape, axis)


def kernel(x_hbm, w_hbm, l_hbm, r_hbm, dl_out, dr_out, loss_out,
           xx, wb, lall, lown, rh, rexp, rexp2, fm, acc, slope, bmt,
           gr, gl, lossv, ggr, ggl, zrr, zrl, s8r, s8l, xrr, xrl, sc, scz, sct, glr, ssem, rsem, lsem):
    d = lax.axis_index("dp")
    t = lax.axis_index("tensor")
    x, z = d % NX, d // NX
    y, core = t // 2, t % 2
    side = ((x + 1) // 2) % 2
    q = x // 2

    def dp_dev(xv, zv):
        return {"dp": zv * NX + xv, "tensor": t}

    def t_dev(tv):
        return {"dp": d, "tensor": tv}

    partner = dp_dev(x + 1 - 2 * (x % 2), z)
    ladder = dp_dev(3 - x, z)
    zdev = (dp_dev(x, (z + 1) % NZ), dp_dev(x, (z + NZ - 1) % NZ))
    ydev = (t_dev((t + 2) % NT), t_dev((t + NT - 2) % NT))
    other = t_dev(t + 1 - 2 * core)

    ids, sends = {}, []

    def rid(key):
        return ids.setdefault(key, len(ids))

    def send(src, dst, key, dev):
        copy = pltpu.make_async_remote_copy(
            src_ref=src, dst_ref=dst, send_sem=ssem.at[len(sends)], recv_sem=rsem.at[rid(key)],
            device_id=dev, device_id_type=MESH)
        copy.start()
        sends.append(copy)

    def recv(ref, key):
        pltpu.make_async_remote_copy(
            src_ref=ref, dst_ref=ref, send_sem=ssem.at[0], recv_sem=rsem.at[rid(key)],
            device_id=ladder, device_id_type=MESH).wait_recv()

    loads = [pltpu.make_async_copy(l_hbm, lall.at[t], lsem.at[0]),
             pltpu.make_async_copy(r_hbm.at[:, pl.ds(pl.multiple_of(side * HC, 128), HC)], rh, lsem.at[1])]
    own_rows = pl.ds(pl.multiple_of(z * KS + x * BK, BK), BK)
    own_w = pltpu.make_async_copy(
        w_hbm.at[:, pl.ds(pl.multiple_of(side * HC, 128), HC)], wb.at[own_rows, :], lsem.at[2])
    own_w.start()
    for c in loads:
        c.start()
    xloads = []
    for k in range(NT):
        c = pltpu.make_async_copy(x_hbm.at[:, :, pl.ds(k * KS, KS)], xx.at[0:NC, k], lsem.at[3 + k])
        c.start()
        xloads.append(c)

    barrier = pltpu.get_barrier_semaphore()
    peers = ([dp_dev((x + k) % NX, z) for k in range(1, NX)]
             + [dp_dev(x, (z + k) % NZ) for k in range(1, NZ)]
             + [t_dev((t + k) % NT) for k in range(1, NT)])
    for dev in peers:
        pl.semaphore_signal(barrier, inc=1, device_id=dev, device_id_type=MESH)
    pl.semaphore_wait(barrier, len(peers))

    def brow(zv, u):
        r = x % 2 if u == 0 else 1 - x % 2
        return pl.ds(pl.multiple_of(zv * KS + q * 256 + r * BK, BK), BK)

    def lbrow(zv, u):
        r = x % 2 if u == 0 else 1 - x % 2
        return pl.ds(pl.multiple_of(zv * KS + (1 - q) * 256 + (1 - r) * BK, BK), BK)

    def arow(zv, v):
        qq = q if v == 0 else 1 - q
        return pl.ds(pl.multiple_of(zv * KS + qq * 256, 256), 256)

    def bref(rows):
        return wb.at[rows, NA:HC]

    def aref(rows):
        return wb.at[rows, 0:NA]

    def zat(o):
        return (z + o + NZ) % NZ

    def hops(direction, first):
        return 4 if direction == (0 if first else 1) else 3

    bcol = pl.ds(pl.multiple_of(side * HC + NA, 128), HC - NA)
    acol = pl.ds(pl.multiple_of(side * HC, 128), NA)
    obcol = pl.ds(pl.multiple_of((1 - side) * HC + NA, 128), HC - NA)
    oacol = pl.ds(pl.multiple_of((1 - side) * HC, 128), NA)

    send(w_hbm.at[:, obcol], bref(own_rows), ("injb",), partner)
    for k in range(1, NT):
        send(l_hbm, lall.at[t], ("l", k), t_dev((t + k) % NT))
    for dr in range(2):
        send(w_hbm.at[:, bcol], bref(own_rows), ("b", dr, 0, 1), zdev[dr])
    send(w_hbm.at[:, bcol], bref(own_rows), ("lb", 0, 0, 0), ladder)
    send(w_hbm.at[:, oacol], aref(own_rows), ("inja",), partner)
    send(w_hbm.at[:, acol], aref(own_rows), ("la", 0), ladder)
    for dr in range(2):
        send(w_hbm.at[:, acol], aref(own_rows), ("a0", dr, 0), zdev[dr])
    for c in range(NC):
        send(x_hbm.at[c, :, pl.ds(pl.multiple_of(t * KS, KS), KS)], xx.at[NC + c, t], ("xc", c), partner)
    far = (t + 4) % NT
    for c in EXTRA:
        send(x_hbm.at[c, :, pl.ds(pl.multiple_of(far * KS, KS), KS)], xx.at[NC + c, far], ("y2", c), partner)

    def zfrom(dr, s):
        return zat(-s if dr == 0 else s)

    def b_step(u, s, dr):
        ref = bref(brow(zfrom(dr, s), u))
        recv(ref, ("b", dr, u, s))
        if s < hops(dr, u == 0):
            send(ref, ref, ("b", dr, u, s + 1), zdev[dr])
        send(ref, ref, ("lb", dr, u, s), ladder)

    def lb_wait(u, s, dr):
        recv(bref(lbrow(zfrom(dr, s), u)), ("lb", dr, u, s))

    def a_step(v, s, dr):
        zv = zfrom(dr, s)
        ref = aref(arow(zv, v))
        if v == 0 and s == 1:
            for u in range(2):
                recv(aref(brow(zv, u)), ("a0", dr, u))
        else:
            recv(ref, ("a", dr, v, s))
        if s < hops(dr, v == 0):
            send(ref, ref, ("a", dr, v, s + 1), zdev[dr])

    def inj_b():
        ref = bref(brow(z, 1))
        recv(ref, ("injb",))
        for dr in range(2):
            send(ref, ref, ("b", dr, 1, 1), zdev[dr])
        send(ref, ref, ("lb", 0, 1, 0), ladder)

    def inj_a():
        ref = aref(brow(z, 1))
        recv(ref, ("inja",))
        send(ref, ref, ("la", 1), ladder)
        for dr in range(2):
            send(ref, ref, ("a0", dr, 1), zdev[dr])

    def lad_a():
        for u in range(2):
            recv(aref(lbrow(z, u)), ("la", u))
        ref = aref(arow(z, 1))
        for dr in range(2):
            send(ref, ref, ("a", dr, 1, 1), zdev[dr])

    def lad_b():
        for u in range(2):
            recv(bref(lbrow(z, u)), ("lb", 0, u, 0))
        own_w.wait()

    def x_cross(c):
        ref = xx.at[NC + c, t]
        recv(ref, ("xc", c))
        for dr in range(2):
            send(ref, ref, ("y", dr, c), ydev[dr])
        send(ref, ref, ("sw", 0, c), other)

    def slice_at(o):
        return (t + 2 * o + NT) % NT

    def x_hop(c, dr):
        ref = xx.at[NC + c, slice_at(-1 if dr == 0 else 1)]
        recv(ref, ("y", dr, c))
        send(ref, ref, ("sw", 1 + dr, c), other)
        if c not in EXTRA and c % 2 == dr:
            send(ref, ref, ("y2", c), ydev[dr])

    def x_far(c):
        ref = xx.at[NC + c, slice_at(2)]
        recv(ref, ("y2", c))
        send(ref, ref, ("sw", 3, c), other)

    def x_swap(c):
        to = 1 - 2 * core
        for k, o in enumerate((0, -1, 1, 2)):
            recv(xx.at[NC + c, (t + to + 2 * o + NT) % NT], ("sw", k, c))

    def first_mix(m0):
        rows = 2 * CH
        for k in range(0, NT, 2):
            a = jnp.concatenate([xx[m0:m0 + 2, k].reshape(rows, KS), xx[m0:m0 + 2, k + 1].reshape(rows, KS)], axis=1)
            p = dot(a, lown[k:k + 2].reshape(2 * KS, NM))
            total = p if k == 0 else total + p
        mixed = total.astype(BF)
        fm[m0:m0 + 2] = mixed.reshape(2, CH, NM)
        acc[m0:m0 + 2] -= dot(mixed, rexp[...]).reshape(2, CH, HC)

    def targets(m_lo, m_n, r_lo, r_n):
        def part(k, carry):
            m0 = m_lo + (k % m_n) * 2
            r = r_lo + k // m_n
            zv = (z + ((r + 1) // 2) * (2 * (r % 2) - 1) + NZ) % NZ
            a = xx[pl.ds(m0, 2), zv].reshape(2 * CH, KS)
            w = wb[pl.ds(pl.multiple_of(zv * KS, KS), KS), :]
            p = dot(a, w).reshape(2, CH, HC)
            if r_lo == 0:
                acc[pl.ds(m0, 2)] = p
            else:
                acc[pl.ds(m0, 2)] += p
            return carry
        lax.fori_loop(0, m_n * r_n, part, 0)

    col_block = iota((NB, HC), 1) // SO

    def expand_right():
        for c in xloads:
            c.wait()
        loads[1].wait()
        for j in range(JB):
            rexp[j * NB:(j + 1) * NB] = jnp.where(col_block == j, rh[...], 0).astype(BF)
        pick = (iota((NM, NB), 0) // JB == iota((NM, NB), 1)).astype(BF)
        spread = dot(pick, rh[...])
        rexp2[...] = jnp.where(iota((NM, HC), 0) % JB == iota((NM, HC), 1) // SO, spread, 0.0).astype(BF)

    def gather_left():
        loads[0].wait()
        for k in range(1, NT):
            recv(lall.at[(t + NT - k) % NT], ("l", k))

    def expand_left():
        first_j = 2 * JB * t + JB * side

        def expand(il, carry):
            row, col = iota((KS, NM), 0), iota((KS, NM), 1)
            choose = jnp.where((row // NB == il) & (row % NB == first_j + col // NB), 1.0, 0.0).astype(BF)
            p = dot(lall[...].reshape(KS, KS), choose)
            keep = col % NB == (row // NB) * 8 + il
            lown[:, il] = jnp.where(keep, p, 0.0).astype(BF).reshape(NT, SI, NM)
            return carry
        lax.fori_loop(0, 8, expand, 0)

    events = {"injb": inj_b, "inja": inj_a, "la": lad_a, "lb0": lad_b, "l": gather_left,
              "rex": expand_right, "exp": expand_left}
    at = 0
    while at < len(ORDER):
        name = ORDER[at]
        at += 1
        nums = [int(ch) for ch in name if ch.isdigit()]
        kind = name.rstrip("0123456789")
        if name in events:
            events[name]()
        elif kind == "f":
            first_mix(2 * nums[0])
        elif kind in ("o", "x") and name[0:2] != "x2" or kind == "x" and len(nums) == 2:
            r, n = nums[-1], 1
            while r and at < len(ORDER) and ORDER[at] == name[:-1] + str(r + n):
                n, at = n + 1, at + 1
            targets(0 if kind == "o" else NC + 2 * nums[0], 2 if kind == "o" else 1, r, n)
        elif kind == "b":
            b_step(*nums)
        elif kind == "lb":
            lb_wait(*nums)
        elif kind == "a":
            a_step(*nums)
        elif kind == "xc":
            x_cross(*nums)
        elif kind == "y":
            x_hop(*nums)
        elif kind == "e":
            x_far(*nums)
        elif kind == "sw":
            x_swap(*nums)
        else:
            raise ValueError(name)

    gr[...] = jnp.zeros_like(gr)
    lossv[...] = jnp.zeros_like(lossv)

    def right_part(p, carry):
        m0 = 2 * p
        a = acc[pl.ds(m0, 2)].reshape(2 * CH, HC)
        lossv[...] += jnp.sum((a * a).reshape(2 * CH // 8, 8, HC), axis=0)
        sl = (a * (-1.0 / TOKENS)).astype(BF)
        slope[p] = sl
        gr[...] += lax.dot_general(fm[pl.ds(m0, 2)].reshape(2 * CH, NM), sl, TN_DIMS, preferred_element_type=F32)
        return carry
    lax.fori_loop(0, 4, right_part, 0)
    right = jnp.zeros((NB, HC), F32)
    for j in range(JB):
        right += jnp.where(col_block == j, gr[j * NB:(j + 1) * NB], 0.0)
    ggr[...] = right

    def rows_of(zv):
        return pl.ds(pl.multiple_of(zv * 8, 8), 8)

    def z_send(src, dst, key):
        for k in range(1, NZ):
            send(src.at[rows_of((z + k) % NZ)], dst.at[k], (key, k), dp_dev(x, (z + k) % NZ))

    def z_sum(src, dst, key, out):
        total = src[rows_of(z), :]
        for k in range(1, NZ):
            recv(dst.at[k], (key, k))
            total += dst[k]
        out[...] = total
        return total

    def x_send(src, dst, key):
        for k in range(1, NX):
            send(src, dst.at[k], (key, k), dp_dev((x + k) % NX, z))

    def x_sum(total, dst, key):
        first = jnp.where(side == 0, total, 0.0)
        second = jnp.where(side == 0, 0.0, total)
        for k in range(1, NX):
            recv(dst.at[k], (key, k))
            from_side = (((x + NX - k) % NX + 1) // 2) % 2
            v = dst[k]
            first += jnp.where(from_side == 0, v, 0.0)
            second += jnp.where(from_side == 0, 0.0, v)
        return first, second

    z_send(ggr, zrr, "zr")

    def back_part(p, carry):
        bmt[p] = lax.dot_general(rexp2[...], slope[p], NT_DIMS, preferred_element_type=F32).astype(BF)
        return carry
    lax.fori_loop(0, 4, back_part, 0)

    def left_part(k, carry):
        rows = pl.ds(pl.multiple_of(k * 32, 32), 32)
        total = dot(bmt[0, rows, :], xx[0:2, k].reshape(2 * CH, KS))
        for p in range(1, 4):
            total += dot(bmt[p, rows, :], xx[2 * p:2 * p + 2, k].reshape(2 * CH, KS))
        gl[k] = total
        return carry
    lax.fori_loop(0, NT, left_part, 0)
    row32 = iota((32, 128), 0)
    folded = []
    for k in range(NT):
        v = jnp.zeros((32, 128), F32)
        for p in range(4):
            v += jnp.where(row32 // 8 == p, gl[k, :, p * 128:(p + 1) * 128], 0.0)
        folded.append(jnp.where((row32 // 4) % 2 == 0, v, pltpu.roll(v, 64, 1)))
    ggl[:, 0:NM] = jnp.transpose(jnp.concatenate(folded, axis=0))[0:SI]
    ggl[:, NM:LW] = jnp.full((NB, 128), jnp.sum(lossv[...]), F32)
    z_send(ggl, zrl, "zl")

    total_r = z_sum(ggr, zrr, "zr", s8r)
    x_send(s8r, xrr, "xr")
    total_l = z_sum(ggl, zrl, "zl", s8l)
    x_send(s8l, xrl, "xl")
    first, second = x_sum(total_r, xrr, "xr")
    sq_right = jnp.sum(first * first + second * second)
    left_a, left_b = x_sum(total_l, xrl, "xl")

    def own(v):
        out = v[0:2]
        for k in range(1, NX):
            out = jnp.where(x == k, v[2 * k:2 * k + 2], out)
        return out

    loss_xz = left_a[:, NM:LW] + left_b[:, NM:LW]
    left_a, left_b = left_a[:, 0:NM], left_b[:, 0:NM]
    sq_left = jnp.sum(left_a * left_a + left_b * left_b)
    srow = iota((8, 128), 0)
    sc[...] = jnp.where(srow == 0, sq_right, jnp.where(srow == 1, sq_left, 0.0))
    for k in range(1, NZ):
        send(sc, scz.at[k], ("sz", k), dp_dev(x, (z + k) % NZ))
    glr[t] = jnp.zeros((8, 2 * NM), F32)
    glr[t, 0:2, 0:NM] = own(left_a)
    glr[t, 0:2, NM:2 * NM] = own(left_b)
    for k in range(1, NT):
        send(glr.at[t], glr.at[t], ("gl", k), t_dev((t + k) % NT))
    lane, col = iota((NM, KS), 0), iota((NM, KS), 1)
    place = jnp.where((lane // JB == 8 * t + col // NB) & (lane % JB == col % JB), 1.0, 0.0)
    for k in range(1, NT):
        recv(glr.at[(t + NT - k) % NT], ("gl", k))
    parts = [glr[k, :, h * NM:(h + 1) * NM] for k in range(NT) for h in range(2)]
    moved = jnp.dot(jnp.concatenate(parts, axis=0), place, precision=lax.Precision.HIGHEST,
                    preferred_element_type=F32)
    mrow, mcol = iota((128, KS), 0), iota((128, KS), 1)
    moved = jnp.where(mrow // 8 == (mcol % NB) // JB, moved, 0.0)
    left_rows = jnp.sum(moved.reshape(16, 8, KS), axis=0)[0:2]
    right_a, right_b = own(first), own(second)
    tot = sc[...]
    for k in range(1, NZ):
        recv(scz.at[k], ("sz", k))
        tot += scz[k]
    tot = jnp.where(srow == 2, loss_xz, tot)
    sct[0] = tot
    for k in range(1, NT):
        send(sct.at[0], sct.at[k], ("st", k), t_dev((t + k) % NT))
    for k in range(1, NT):
        recv(sct.at[k], ("st", k))
        tot += sct[k]
    scale_right = lax.rsqrt(tot[0:1, 0:1] / (NB * F) + EPS)
    scale_left = lax.rsqrt(tot[1:2, 0:1] / (SI * MID) + EPS)
    dr_out[:, 0:HC] = right_a * scale_right
    dr_out[:, HC:2 * HC] = right_b * scale_right
    dl_out[...] = left_rows * scale_left
    loss_out[...] = tot[2:3, :] / (2.0 * TOKENS)
    for copy in sends:
        copy.wait_send()


def local(tokens, dense_weight, left_factor, right_factor):
    vmem = pl.BlockSpec(memory_space=pltpu.VMEM)
    hbm = pl.BlockSpec(memory_space=pl.ANY)
    dir_left, dir_right, loss = pl.pallas_call(
        kernel,
        out_shape=(jax.ShapeDtypeStruct((2, KS), F32),
                   jax.ShapeDtypeStruct((2, 2 * HC), F32),
                   jax.ShapeDtypeStruct((1, 128), F32)),
        in_specs=[hbm] * 4,
        out_specs=(vmem,) * 3,
        scratch_shapes=[
            pltpu.VMEM((2 * NC, NT, CH, KS), BF),
            pltpu.VMEM((4096, HC), BF),
            pltpu.VMEM((NT, SI, KS), BF),
            pltpu.VMEM((NT, 8, SI, NM), BF),
            pltpu.VMEM((NB, HC), BF),
            pltpu.VMEM((NM, HC), BF),
            pltpu.VMEM((NM, HC), BF),
            pltpu.VMEM((2 * NC, CH, NM), BF),
            pltpu.VMEM((2 * NC, CH, HC), F32),
            pltpu.VMEM((NC, 2 * CH, HC), BF),
            pltpu.VMEM((NC, NM, 2 * CH), BF),
            pltpu.VMEM((NM, HC), F32),
            pltpu.VMEM((NT, 32, KS), F32),
            pltpu.VMEM((8, HC), F32),
            pltpu.VMEM((NB, HC), F32),
            pltpu.VMEM((NB, LW), F32),
            pltpu.VMEM((NZ, 8, HC), F32),
            pltpu.VMEM((NZ, 8, LW), F32),
            pltpu.VMEM((8, HC), F32),
            pltpu.VMEM((8, LW), F32),
            pltpu.VMEM((NX, 8, HC), F32),
            pltpu.VMEM((NX, 8, LW), F32),
            pltpu.VMEM((8, 128), F32),
            pltpu.VMEM((NZ, 8, 128), F32),
            pltpu.VMEM((NT, 8, 128), F32),
            pltpu.VMEM((NT, 8, 2 * NM), F32),
            pltpu.SemaphoreType.DMA((160,)),
            pltpu.SemaphoreType.DMA((160,)),
            pltpu.SemaphoreType.DMA((16,)),
        ],
        compiler_params=pltpu.CompilerParams(
            collective_id=0, has_side_effects=True, vmem_limit_bytes=60 * 1024 * 1024),
    )(tokens.reshape(NC, CH, 4096), dense_weight, left_factor, right_factor)
    return (dir_left, dir_right, loss[0, 0])


def solution(mesh):
    in_specs = (P("dp", None), P("dp", "tensor"), P(None, "tensor"), P(None, "tensor"))
    out_specs = (P("dp", "tensor"), P("dp", "tensor"), P())
    return jax.shard_map(local, mesh=mesh, in_specs=in_specs, out_specs=out_specs, check_vma=False)
```

```python
import jax
import jax.numpy as jnp
from jax import lax
from jax.experimental import pallas as pl
from jax.experimental.pallas import tpu as pltpu
from jax.sharding import PartitionSpec as P

MESH = pl.DeviceIdType.MESH
F = 14336
NB = 64
SI = 64
SO = 224
MID = 4096
TOKENS = 30720
EPS = 1e-06

NX, NZ, NT = 4, 8, 8
CH = 240
NC = 4
KS = 512
HC = 896
NA = 384
BK = 128
JB = 4
NM = JB * NB
RW = HC + 128
BF = jnp.bfloat16
F32 = jnp.float32
NT_DIMS = (((1,), (1,)), ((), ()))
TN_DIMS = (((0,), (0,)), ((), ()))
EXTRA = (2, 3)
ORDER = (
    "rex", "l", "exp", "injb", "b010", "b011", "inja", "b110", "b111", "lb0", "xc0", "b020", "b021", "lb010",
    "a010", "a011", "lb011", "xc1", "la", "b120", "b121", "o0", "y00", "y01", "f0", "b030", "b031", "xc2",
    "lb110", "f1", "y10", "y11", "lb111", "a020", "a021", "lb020", "xc3", "e0", "y21", "lb021", "a110",
    "a111", "o1", "sw0", "o2", "b130", "b131", "lb120", "e2", "y20", "e1", "lb121", "b040", "sw2", "sw1",
    "a031", "x00", "x01", "lb030", "x02", "e3", "f2", "a030", "y30", "y31", "a121", "lb031", "o3", "x03",
    "a120", "b141", "sw3", "lb130", "x10", "x11", "x12", "x13", "lb131", "o4", "a131", "a040", "x04", "x14",
    "lb040", "o5", "x05", "x15", "lb141", "a130", "o6", "x06", "a141", "x16", "o7", "x07", "x17", "f3")


def dot(a, b):
    return jnp.dot(a, b, preferred_element_type=F32)


def iota(shape, axis):
    return lax.broadcasted_iota(jnp.int32, shape, axis)


def kernel(x_hbm, w_hbm, l_hbm, r_hbm, dl_out, dr_out, loss_out,
           xx, wb, lraw, lpack, lall, lown, rh, rexp, rexp2, fm, acc, slope, bmt,
           gr, gl, lossv, ggr, ggl, zrr, zrl, s8r, s8l, xrr, xrl, s8f, xrf, sc, scz, sct, glr, ssem, rsem, lsem):
    d = lax.axis_index("dp")
    t = lax.axis_index("tensor")
    x, z = d % NX, d // NX
    y, core = t // 2, t % 2
    side = ((x + 1) // 2) % 2
    q = x // 2

    def dp_dev(xv, zv):
        return {"dp": zv * NX + xv, "tensor": t}

    def t_dev(tv):
        return {"dp": d, "tensor": tv}

    partner = dp_dev(x + 1 - 2 * (x % 2), z)
    ladder = dp_dev(3 - x, z)
    zdev = (dp_dev(x, (z + 1) % NZ), dp_dev(x, (z + NZ - 1) % NZ))
    ydev = (t_dev((t + 2) % NT), t_dev((t + NT - 2) % NT))
    other = t_dev(t + 1 - 2 * core)

    ids, sends = {}, []

    def rid(key):
        return ids.setdefault(key, len(ids))

    def send(src, dst, key, dev):
        copy = pltpu.make_async_remote_copy(
            src_ref=src, dst_ref=dst, send_sem=ssem.at[len(sends)], recv_sem=rsem.at[rid(key)],
            device_id=dev, device_id_type=MESH)
        copy.start()
        sends.append(copy)

    def recv(ref, key):
        pltpu.make_async_remote_copy(
            src_ref=ref, dst_ref=ref, send_sem=ssem.at[0], recv_sem=rsem.at[rid(key)],
            device_id=ladder, device_id_type=MESH).wait_recv()

    loads = [pltpu.make_async_copy(l_hbm, lraw, lsem.at[0]),
             pltpu.make_async_copy(r_hbm.at[:, pl.ds(pl.multiple_of(side * HC, 128), HC)], rh, lsem.at[1])]
    own_rows = pl.ds(pl.multiple_of(z * KS + x * BK, BK), BK)
    own_w = pltpu.make_async_copy(
        w_hbm.at[:, pl.ds(pl.multiple_of(side * HC, 128), HC)], wb.at[own_rows, :], lsem.at[2])
    own_w.start()
    for c in loads:
        c.start()
    xloads = []
    for k in range(NT):
        c = pltpu.make_async_copy(x_hbm.at[:, :, pl.ds(k * KS, KS)], xx.at[0:NC, k], lsem.at[3 + k])
        c.start()
        xloads.append(c)

    barrier = pltpu.get_barrier_semaphore()
    px = x + 1 - 2 * (x % 2)
    peers = ([ladder] + [dp_dev(px, (z + k) % NZ) for k in range(NZ)]
             + [dp_dev(x, (z + k) % NZ) for k in range(1, NZ)]
             + [t_dev((t + k) % NT) for k in range(1, NT)])
    for dev in peers:
        pl.semaphore_signal(barrier, inc=1, device_id=dev, device_id_type=MESH)
    for c in loads:
        c.wait()
    lrow, lcol = iota((KS, BK), 0), iota((KS, BK), 1)
    for k in range(NT):
        take = jnp.where((lcol < 64) & (lrow // NB == lcol // 8) & (lrow % NB == 8 * k + lcol % 8), 1.0, 0.0)
        lpack[k] = dot(lraw[...], take.astype(BF)).astype(BF)
    pl.semaphore_wait(barrier, len(peers))

    def brow(zv, u):
        r = x % 2 if u == 0 else 1 - x % 2
        return pl.ds(pl.multiple_of(zv * KS + q * 256 + r * BK, BK), BK)

    def lbrow(zv, u):
        r = x % 2 if u == 0 else 1 - x % 2
        return pl.ds(pl.multiple_of(zv * KS + (1 - q) * 256 + (1 - r) * BK, BK), BK)

    def arow(zv, v):
        qq = q if v == 0 else 1 - q
        return pl.ds(pl.multiple_of(zv * KS + qq * 256, 256), 256)

    def bref(rows):
        return wb.at[rows, NA:HC]

    def aref(rows):
        return wb.at[rows, 0:NA]

    def zat(o):
        return (z + o + NZ) % NZ

    def hops(direction, first):
        return 4 if direction == (0 if first else 1) else 3

    bcol = pl.ds(pl.multiple_of(side * HC + NA, 128), HC - NA)
    acol = pl.ds(pl.multiple_of(side * HC, 128), NA)
    obcol = pl.ds(pl.multiple_of((1 - side) * HC + NA, 128), HC - NA)
    oacol = pl.ds(pl.multiple_of((1 - side) * HC, 128), NA)

    send(w_hbm.at[:, obcol], bref(own_rows), ("injb",), partner)
    for k in range(1, NT):
        send(lpack.at[(t + k) % NT], lall.at[t], ("l", k), t_dev((t + k) % NT))
    for dr in range(2):
        send(w_hbm.at[:, bcol], bref(own_rows), ("b", dr, 0, 1), zdev[dr])
    send(w_hbm.at[:, bcol], bref(own_rows), ("lb", 0, 0, 0), ladder)
    send(w_hbm.at[:, oacol], aref(own_rows), ("inja",), partner)
    send(w_hbm.at[:, acol], aref(own_rows), ("la", 0), ladder)
    for dr in range(2):
        send(w_hbm.at[:, acol], aref(own_rows), ("a0", dr, 0), zdev[dr])
    for c in range(NC):
        send(x_hbm.at[c, :, pl.ds(pl.multiple_of(t * KS, KS), KS)], xx.at[NC + c, t], ("xc", c), partner)
    far = (t + 4) % NT
    for c in EXTRA:
        send(x_hbm.at[c, :, pl.ds(pl.multiple_of(far * KS, KS), KS)], xx.at[NC + c, far], ("y2", c), partner)

    def zfrom(dr, s):
        return zat(-s if dr == 0 else s)

    def b_step(u, s, dr):
        ref = bref(brow(zfrom(dr, s), u))
        recv(ref, ("b", dr, u, s))
        if s < hops(dr, u == 0):
            send(ref, ref, ("b", dr, u, s + 1), zdev[dr])
        send(ref, ref, ("lb", dr, u, s), ladder)

    def lb_wait(u, s, dr):
        recv(bref(lbrow(zfrom(dr, s), u)), ("lb", dr, u, s))

    def a_step(v, s, dr):
        zv = zfrom(dr, s)
        ref = aref(arow(zv, v))
        if v == 0 and s == 1:
            for u in range(2):
                recv(aref(brow(zv, u)), ("a0", dr, u))
        else:
            recv(ref, ("a", dr, v, s))
        if s < hops(dr, v == 0):
            send(ref, ref, ("a", dr, v, s + 1), zdev[dr])

    def inj_b():
        ref = bref(brow(z, 1))
        recv(ref, ("injb",))
        for dr in range(2):
            send(ref, ref, ("b", dr, 1, 1), zdev[dr])
        send(ref, ref, ("lb", 0, 1, 0), ladder)

    def inj_a():
        ref = aref(brow(z, 1))
        recv(ref, ("inja",))
        send(ref, ref, ("la", 1), ladder)
        for dr in range(2):
            send(ref, ref, ("a0", dr, 1), zdev[dr])

    def lad_a():
        for u in range(2):
            recv(aref(lbrow(z, u)), ("la", u))
        ref = aref(arow(z, 1))
        for dr in range(2):
            send(ref, ref, ("a", dr, 1, 1), zdev[dr])

    def lad_b():
        for u in range(2):
            recv(bref(lbrow(z, u)), ("lb", 0, u, 0))
        own_w.wait()

    def x_cross(c):
        ref = xx.at[NC + c, t]
        recv(ref, ("xc", c))
        for dr in range(2):
            send(ref, ref, ("y", dr, c), ydev[dr])
        send(ref, ref, ("sw", 0, c), other)

    def slice_at(o):
        return (t + 2 * o + NT) % NT

    def x_hop(c, dr):
        ref = xx.at[NC + c, slice_at(-1 if dr == 0 else 1)]
        recv(ref, ("y", dr, c))
        send(ref, ref, ("sw", 1 + dr, c), other)
        if c not in EXTRA and c % 2 == dr:
            send(ref, ref, ("y2", c), ydev[dr])

    def x_far(c):
        ref = xx.at[NC + c, slice_at(2)]
        recv(ref, ("y2", c))
        send(ref, ref, ("sw", 3, c), other)

    def x_swap(c):
        to = 1 - 2 * core
        for k, o in enumerate((0, -1, 1, 2)):
            recv(xx.at[NC + c, (t + to + 2 * o + NT) % NT], ("sw", k, c))

    def first_mix(m0):
        rows = 2 * CH
        for k in range(0, NT, 2):
            a = jnp.concatenate([xx[m0:m0 + 2, k].reshape(rows, KS), xx[m0:m0 + 2, k + 1].reshape(rows, KS)], axis=1)
            p = dot(a, lown[k:k + 2].reshape(2 * KS, NM))
            total = p if k == 0 else total + p
        mixed = total.astype(BF)
        fm[m0:m0 + 2] = mixed.reshape(2, CH, NM)
        acc[m0:m0 + 2] -= dot(mixed, rexp[...]).reshape(2, CH, HC)

    def targets(m_lo, m_n, r_lo, r_n):
        def part(k, carry):
            m0 = m_lo + (k % m_n) * 2
            r = r_lo + k // m_n
            zv = (z + ((r + 1) // 2) * (2 * (r % 2) - 1) + NZ) % NZ
            a = xx[pl.ds(m0, 2), zv].reshape(2 * CH, KS)
            w = wb[pl.ds(pl.multiple_of(zv * KS, KS), KS), :]
            p = dot(a, w).reshape(2, CH, HC)
            if r_lo == 0:
                acc[pl.ds(m0, 2)] = p
            else:
                acc[pl.ds(m0, 2)] += p
            return carry
        lax.fori_loop(0, m_n * r_n, part, 0)

    col_block = iota((NB, HC), 1) // SO

    def expand_right():
        for c in xloads:
            c.wait()
        for j in range(JB):
            rexp[j * NB:(j + 1) * NB] = jnp.where(col_block == j, rh[...], 0).astype(BF)
        pick = (iota((NM, NB), 0) // JB == iota((NM, NB), 1)).astype(BF)
        spread = dot(pick, rh[...])
        rexp2[...] = jnp.where(iota((NM, HC), 0) % JB == iota((NM, HC), 1) // SO, spread, 0.0).astype(BF)

    def gather_left():
        for k in range(1, NT):
            recv(lall.at[(t + NT - k) % NT], ("l", k))
        lall[t] = lpack[t]

    def expand_left():
        def expand(il, carry):
            row, col = iota((BK, NM), 0), iota((BK, NM), 1)
            choose = jnp.where((row // 8 == il) & (row % 8 == JB * side + col // NB), 1.0, 0.0).astype(BF)
            p = dot(lall[...].reshape(KS, BK), choose)
            row, col = iota((KS, NM), 0), iota((KS, NM), 1)
            keep = col % NB == (row // NB) * 8 + il
            lown[:, il] = jnp.where(keep, p, 0.0).astype(BF).reshape(NT, SI, NM)
            return carry
        lax.fori_loop(0, 8, expand, 0)

    events = {"injb": inj_b, "inja": inj_a, "la": lad_a, "lb0": lad_b, "l": gather_left,
              "rex": expand_right, "exp": expand_left}
    at = 0
    while at < len(ORDER):
        name = ORDER[at]
        at += 1
        nums = [int(ch) for ch in name if ch.isdigit()]
        kind = name.rstrip("0123456789")
        if name in events:
            events[name]()
        elif kind == "f":
            first_mix(2 * nums[0])
        elif kind in ("o", "x") and name[0:2] != "x2" or kind == "x" and len(nums) == 2:
            r, n = nums[-1], 1
            while r and at < len(ORDER) and ORDER[at] == name[:-1] + str(r + n):
                n, at = n + 1, at + 1
            targets(0 if kind == "o" else NC + 2 * nums[0], 2 if kind == "o" else 1, r, n)
        elif kind == "b":
            b_step(*nums)
        elif kind == "lb":
            lb_wait(*nums)
        elif kind == "a":
            a_step(*nums)
        elif kind == "xc":
            x_cross(*nums)
        elif kind == "y":
            x_hop(*nums)
        elif kind == "e":
            x_far(*nums)
        elif kind == "sw":
            x_swap(*nums)
        else:
            raise ValueError(name)

    gr[...] = jnp.zeros_like(gr)
    lossv[...] = jnp.zeros_like(lossv)

    def right_part(p, carry):
        m0 = 2 * p
        a = acc[pl.ds(m0, 2)].reshape(2 * CH, HC)
        lossv[...] += jnp.sum((a * a).reshape(2 * CH // 8, 8, HC), axis=0)
        sl = (a * (-1.0 / TOKENS)).astype(BF)
        slope[p] = sl
        gr[...] += lax.dot_general(fm[pl.ds(m0, 2)].reshape(2 * CH, NM), sl, TN_DIMS, preferred_element_type=F32)
        return carry
    lax.fori_loop(0, 4, right_part, 0)
    right = jnp.zeros((NB, HC), F32)
    for j in range(JB):
        right += jnp.where(col_block == j, gr[j * NB:(j + 1) * NB], 0.0)
    ggr[:, 0:HC] = right
    ggr[:, HC:RW] = jnp.full((NB, 128), jnp.sum(lossv[...]) / NZ, F32)

    def rows_of(zv):
        return pl.ds(pl.multiple_of(zv * 8, 8), 8)

    def z_send(src, dst, key):
        for k in range(1, NZ):
            send(src.at[rows_of((z + k) % NZ)], dst.at[k], (key, k), dp_dev(x, (z + k) % NZ))

    def z_sum(src, dst, key, out):
        total = src[rows_of(z), :]
        for k in range(1, NZ):
            recv(dst.at[k], (key, k))
            total += dst[k]
        out[...] = total
        return total

    z_send(ggr, zrr, "zr")

    def back_part(p, carry):
        bmt[p] = lax.dot_general(rexp2[...], slope[p], NT_DIMS, preferred_element_type=F32).astype(BF)
        return carry
    lax.fori_loop(0, 4, back_part, 0)

    def left_part(k, carry):
        rows = pl.ds(pl.multiple_of(k * 32, 32), 32)
        total = dot(bmt[0, rows, :], xx[0:2, k].reshape(2 * CH, KS))
        for p in range(1, 4):
            total += dot(bmt[p, rows, :], xx[2 * p:2 * p + 2, k].reshape(2 * CH, KS))
        gl[k] = total
        return carry
    lax.fori_loop(0, NT, left_part, 0)
    row32 = iota((32, 128), 0)
    folded = []
    for k in range(NT):
        v = jnp.zeros((32, 128), F32)
        for p in range(4):
            v += jnp.where(row32 // 8 == p, gl[k, :, p * 128:(p + 1) * 128], 0.0)
        folded.append(jnp.where((row32 // 4) % 2 == 0, v, pltpu.roll(v, 64, 1)))
    ggl[...] = jnp.transpose(jnp.concatenate(folded, axis=0))[0:SI]
    z_send(ggl, zrl, "zl")

    total_r = z_sum(ggr, zrr, "zr", s8r)
    send(s8r, xrr, ("xr",), ladder)
    total_l = z_sum(ggl, zrl, "zl", s8l)
    send(s8l, xrl, ("xl",), ladder)
    recv(xrr, ("xr",))
    full_r = total_r + xrr[...]
    loss_part = full_r[:, HC:RW]
    full_r = full_r[:, 0:HC]
    sq_right = jnp.sum(full_r * full_r)
    recv(xrl, ("xl",))
    full_l = total_l + xrl[...]
    sq_left = jnp.sum(full_l * full_l)
    srow = iota((8, 128), 0)
    tot = jnp.where(srow == 0, sq_right, jnp.where(srow == 1, sq_left, jnp.where(srow == 2, loss_part, 0.0)))
    sc[...] = tot
    for k in range(NZ):
        if k:
            send(sc, scz.at[k], ("sz", k), dp_dev(x, (z + k) % NZ))
        send(sc, scz.at[NZ + k], ("sz", NZ + k), dp_dev(px, (z + k) % NZ))
    s8f[:, 0:HC] = full_r
    s8f[:, HC:HC + NM] = full_l
    send(s8f, xrf, ("xf",), partner)

    def own(v):
        out = v[0:2]
        for k in range(1, NX):
            out = jnp.where(x == k, v[2 * k:2 * k + 2], out)
        return out

    recv(xrf, ("xf",))
    mine, theirs = own(s8f[...]), own(xrf[...])
    rows_a = jnp.where(side == 0, mine, theirs)
    rows_b = jnp.where(side == 0, theirs, mine)
    glr[t] = jnp.zeros((8, 2 * NM), F32)
    glr[t, 0:2, 0:NM] = rows_a[:, HC:HC + NM]
    glr[t, 0:2, NM:2 * NM] = rows_b[:, HC:HC + NM]
    for k in range(1, NT):
        send(glr.at[t], glr.at[t], ("gl", k), t_dev((t + k) % NT))
    for k in range(1, 2 * NZ):
        recv(scz.at[k], ("sz", k))
        tot += scz[k]
    sct[0] = tot
    for k in range(1, NT):
        send(sct.at[0], sct.at[k], ("st", k), t_dev((t + k) % NT))
    lane, col = iota((NM, KS), 0), iota((NM, KS), 1)
    place = jnp.where((lane // JB == 8 * t + col // NB) & (lane % JB == col % JB), 1.0, 0.0)
    for k in range(1, NT):
        recv(glr.at[(t + NT - k) % NT], ("gl", k))
    parts = [glr[k, :, h * NM:(h + 1) * NM] for k in range(NT) for h in range(2)]
    moved = jnp.dot(jnp.concatenate(parts, axis=0), place, precision=lax.Precision.HIGHEST,
                    preferred_element_type=F32)
    mrow, mcol = iota((128, KS), 0), iota((128, KS), 1)
    moved = jnp.where(mrow // 8 == (mcol % NB) // JB, moved, 0.0)
    left_rows = jnp.sum(moved.reshape(16, 8, KS), axis=0)[0:2]
    for k in range(1, NT):
        recv(sct.at[k], ("st", k))
        tot += sct[k]
    scale_right = lax.rsqrt(tot[0:1, 0:1] / (NB * F) + EPS)
    scale_left = lax.rsqrt(tot[1:2, 0:1] / (SI * MID) + EPS)
    dr_out[:, 0:HC] = rows_a[:, 0:HC] * scale_right
    dr_out[:, HC:2 * HC] = rows_b[:, 0:HC] * scale_right
    dl_out[...] = left_rows * scale_left
    loss_out[...] = tot[2:3, :] / (2.0 * TOKENS)
    for copy in sends:
        copy.wait_send()


def local(tokens, dense_weight, left_factor, right_factor):
    vmem = pl.BlockSpec(memory_space=pltpu.VMEM)
    hbm = pl.BlockSpec(memory_space=pl.ANY)
    dir_left, dir_right, loss = pl.pallas_call(
        kernel,
        out_shape=(jax.ShapeDtypeStruct((2, KS), F32),
                   jax.ShapeDtypeStruct((2, 2 * HC), F32),
                   jax.ShapeDtypeStruct((1, 128), F32)),
        in_specs=[hbm] * 4,
        out_specs=(vmem,) * 3,
        scratch_shapes=[
            pltpu.VMEM((2 * NC, NT, CH, KS), BF),
            pltpu.VMEM((4096, HC), BF),
            pltpu.VMEM((SI, KS), BF),
            pltpu.VMEM((NT, SI, BK), BF),
            pltpu.VMEM((NT, SI, BK), BF),
            pltpu.VMEM((NT, 8, SI, NM), BF),
            pltpu.VMEM((NB, HC), BF),
            pltpu.VMEM((NM, HC), BF),
            pltpu.VMEM((NM, HC), BF),
            pltpu.VMEM((2 * NC, CH, NM), BF),
            pltpu.VMEM((2 * NC, CH, HC), F32),
            pltpu.VMEM((NC, 2 * CH, HC), BF),
            pltpu.VMEM((NC, NM, 2 * CH), BF),
            pltpu.VMEM((NM, HC), F32),
            pltpu.VMEM((NT, 32, KS), F32),
            pltpu.VMEM((8, HC), F32),
            pltpu.VMEM((NB, RW), F32),
            pltpu.VMEM((NB, NM), F32),
            pltpu.VMEM((NZ, 8, RW), F32),
            pltpu.VMEM((NZ, 8, NM), F32),
            pltpu.VMEM((8, RW), F32),
            pltpu.VMEM((8, NM), F32),
            pltpu.VMEM((8, RW), F32),
            pltpu.VMEM((8, NM), F32),
            pltpu.VMEM((8, HC + NM), F32),
            pltpu.VMEM((8, HC + NM), F32),
            pltpu.VMEM((8, 128), F32),
            pltpu.VMEM((2 * NZ, 8, 128), F32),
            pltpu.VMEM((NT, 8, 128), F32),
            pltpu.VMEM((NT, 8, 2 * NM), F32),
            pltpu.SemaphoreType.DMA((176,)),
            pltpu.SemaphoreType.DMA((176,)),
            pltpu.SemaphoreType.DMA((16,)),
        ],
        compiler_params=pltpu.CompilerParams(
            collective_id=0, has_side_effects=True, vmem_limit_bytes=60 * 1024 * 1024),
    )(tokens.reshape(NC, CH, 4096), dense_weight, left_factor, right_factor)
    return (dir_left, dir_right, loss[0, 0])


def solution(mesh):
    in_specs = (P("dp", None), P("dp", "tensor"), P(None, "tensor"), P(None, "tensor"))
    out_specs = (P("dp", "tensor"), P("dp", "tensor"), P())
    return jax.shard_map(local, mesh=mesh, in_specs=in_specs, out_specs=out_specs, check_vma=False)
```

```python
import jax
import jax.numpy as jnp
from jax import lax
from jax.experimental import pallas as pl
from jax.experimental.pallas import tpu as pltpu
from jax.sharding import PartitionSpec as P

MESH = pl.DeviceIdType.MESH
F = 14336
NB = 64
SI = 64
SO = 224
MID = 4096
TOKENS = 30720
EPS = 1e-06

NX, NZ, NT = 4, 8, 8
CH = 240
NC = 4
KS = 512
HC = 896
NA = 384
BK = 128
JB = 4
NM = JB * NB
RW = HC + 128
BF = jnp.bfloat16
F32 = jnp.float32
NT_DIMS = (((1,), (1,)), ((), ()))
TN_DIMS = (((0,), (0,)), ((), ()))
EXTRA = (2, 3)
ORDER = (
    "rex", "l", "exp", "injb", "b010", "b011", "t0", "inja", "t1", "b110", "b111", "lb0", "xc0", "b020",
    "b021", "lb010", "a010", "a011", "lb011", "xc1", "la", "b120", "b121", "o0", "y00", "y01", "f0", "b030",
    "b031", "lb110", "xc2", "f1", "y10", "y11", "a020", "a021", "lb111", "lb020", "xc3", "lb021", "a110",
    "a111", "o1", "e0", "y21", "o2", "b130", "b131", "lb120", "sw0", "e2", "lb121", "b040", "y20", "e1",
    "a031", "sw2", "sw1", "x00", "x01", "lb030", "x02", "e3", "a030", "y30", "y31", "lb031", "a121", "o3",
    "sw3", "x10", "x11", "a120", "b141", "lb130", "m0", "x12", "x03", "x13", "o4", "lb131", "x04", "a131",
    "a040", "x14", "lb040", "m1", "o5", "x05", "x15", "lb141", "a130", "o6", "x06", "a141", "x16", "o7",
    "x07", "x17", "g0", "g1")


def dot(a, b):
    return jnp.dot(a, b, preferred_element_type=F32)


def iota(shape, axis):
    return lax.broadcasted_iota(jnp.int32, shape, axis)


def kernel(x_hbm, w_hbm, l_hbm, r_hbm, dl_out, dr_out, loss_out,
           xx, wb, lraw, lpack, lall, lown, rh, rexp, rexp2, fm, fmo, acc, slope, bmt,
           gr, gl, lossv, ggr, ggl, zrr, zrl, s8r, s8l, xrr, xrl, s8f, xrf, sc, scz, sct, glr, ssem, rsem, lsem):
    d = lax.axis_index("dp")
    t = lax.axis_index("tensor")
    x, z = d % NX, d // NX
    y, core = t // 2, t % 2
    side = ((x + 1) // 2) % 2
    q = x // 2

    def dp_dev(xv, zv):
        return {"dp": zv * NX + xv, "tensor": t}

    def t_dev(tv):
        return {"dp": d, "tensor": tv}

    partner = dp_dev(x + 1 - 2 * (x % 2), z)
    ladder = dp_dev(3 - x, z)
    zdev = (dp_dev(x, (z + 1) % NZ), dp_dev(x, (z + NZ - 1) % NZ))
    ydev = (t_dev((t + 2) % NT), t_dev((t + NT - 2) % NT))
    other = t_dev(t + 1 - 2 * core)

    ids, sends = {}, []

    def rid(key):
        return ids.setdefault(key, len(ids))

    def send(src, dst, key, dev):
        copy = pltpu.make_async_remote_copy(
            src_ref=src, dst_ref=dst, send_sem=ssem.at[len(sends)], recv_sem=rsem.at[rid(key)],
            device_id=dev, device_id_type=MESH)
        copy.start()
        sends.append(copy)

    def recv(ref, key):
        pltpu.make_async_remote_copy(
            src_ref=ref, dst_ref=ref, send_sem=ssem.at[0], recv_sem=rsem.at[rid(key)],
            device_id=ladder, device_id_type=MESH).wait_recv()

    loads = [pltpu.make_async_copy(l_hbm, lraw, lsem.at[0]),
             pltpu.make_async_copy(r_hbm.at[:, pl.ds(pl.multiple_of(side * HC, 128), HC)], rh, lsem.at[1])]
    own_rows = pl.ds(pl.multiple_of(z * KS + x * BK, BK), BK)
    own_w = pltpu.make_async_copy(
        w_hbm.at[:, pl.ds(pl.multiple_of(side * HC, 128), HC)], wb.at[own_rows, :], lsem.at[2])
    own_w.start()
    for c in loads:
        c.start()
    xloads = []
    for k in range(NT):
        c = pltpu.make_async_copy(x_hbm.at[:, :, pl.ds(k * KS, KS)], xx.at[0:NC, k], lsem.at[3 + k])
        c.start()
        xloads.append(c)

    barrier = pltpu.get_barrier_semaphore()
    px = x + 1 - 2 * (x % 2)
    peers = ([ladder] + [dp_dev(px, (z + k) % NZ) for k in range(NZ)]
             + [dp_dev(x, (z + k) % NZ) for k in range(1, NZ)]
             + [t_dev((t + k) % NT) for k in range(1, NT)])
    for dev in peers:
        pl.semaphore_signal(barrier, inc=1, device_id=dev, device_id_type=MESH)
    for c in loads:
        c.wait()
    lrow, lcol = iota((KS, BK), 0), iota((KS, BK), 1)
    for k in range(NT):
        take = jnp.where((lcol < 64) & (lrow // NB == lcol // 8) & (lrow % NB == 8 * k + lcol % 8), 1.0, 0.0)
        lpack[k] = dot(lraw[...], take.astype(BF)).astype(BF)
    pl.semaphore_wait(barrier, len(peers))

    def brow(zv, u):
        r = x % 2 if u == 0 else 1 - x % 2
        return pl.ds(pl.multiple_of(zv * KS + q * 256 + r * BK, BK), BK)

    def lbrow(zv, u):
        r = x % 2 if u == 0 else 1 - x % 2
        return pl.ds(pl.multiple_of(zv * KS + (1 - q) * 256 + (1 - r) * BK, BK), BK)

    def arow(zv, v):
        qq = q if v == 0 else 1 - q
        return pl.ds(pl.multiple_of(zv * KS + qq * 256, 256), 256)

    def bref(rows):
        return wb.at[rows, NA:HC]

    def aref(rows):
        return wb.at[rows, 0:NA]

    def zat(o):
        return (z + o + NZ) % NZ

    def hops(direction, first):
        return 4 if direction == (0 if first else 1) else 3

    bcol = pl.ds(pl.multiple_of(side * HC + NA, 128), HC - NA)
    acol = pl.ds(pl.multiple_of(side * HC, 128), NA)
    obcol = pl.ds(pl.multiple_of((1 - side) * HC + NA, 128), HC - NA)
    oacol = pl.ds(pl.multiple_of((1 - side) * HC, 128), NA)

    send(w_hbm.at[:, obcol], bref(own_rows), ("injb",), partner)
    for k in range(1, NT):
        send(lpack.at[(t + k) % NT], lall.at[t], ("l", k), t_dev((t + k) % NT))
    for dr in range(2):
        send(w_hbm.at[:, bcol], bref(own_rows), ("b", dr, 0, 1), zdev[dr])
    send(w_hbm.at[:, bcol], bref(own_rows), ("lb", 0, 0, 0), ladder)
    send(w_hbm.at[:, oacol], aref(own_rows), ("inja",), partner)
    send(w_hbm.at[:, acol], aref(own_rows), ("la", 0), ladder)
    for dr in range(2):
        send(w_hbm.at[:, acol], aref(own_rows), ("a0", dr, 0), zdev[dr])
    for c in range(NC):
        send(x_hbm.at[c, :, pl.ds(pl.multiple_of(t * KS, KS), KS)], xx.at[NC + c, t], ("xc", c), partner)
    far = (t + 4) % NT
    for c in EXTRA:
        send(x_hbm.at[c, :, pl.ds(pl.multiple_of(far * KS, KS), KS)], xx.at[NC + c, far], ("y2", c), partner)

    def zfrom(dr, s):
        return zat(-s if dr == 0 else s)

    def b_step(u, s, dr):
        ref = bref(brow(zfrom(dr, s), u))
        recv(ref, ("b", dr, u, s))
        if s < hops(dr, u == 0):
            send(ref, ref, ("b", dr, u, s + 1), zdev[dr])
        send(ref, ref, ("lb", dr, u, s), ladder)

    def lb_wait(u, s, dr):
        recv(bref(lbrow(zfrom(dr, s), u)), ("lb", dr, u, s))

    def a_step(v, s, dr):
        zv = zfrom(dr, s)
        ref = aref(arow(zv, v))
        if v == 0 and s == 1:
            for u in range(2):
                recv(aref(brow(zv, u)), ("a0", dr, u))
        else:
            recv(ref, ("a", dr, v, s))
        if s < hops(dr, v == 0):
            send(ref, ref, ("a", dr, v, s + 1), zdev[dr])

    def inj_b():
        ref = bref(brow(z, 1))
        recv(ref, ("injb",))
        for dr in range(2):
            send(ref, ref, ("b", dr, 1, 1), zdev[dr])
        send(ref, ref, ("lb", 0, 1, 0), ladder)

    def inj_a():
        ref = aref(brow(z, 1))
        recv(ref, ("inja",))
        send(ref, ref, ("la", 1), ladder)
        for dr in range(2):
            send(ref, ref, ("a0", dr, 1), zdev[dr])

    def lad_a():
        for u in range(2):
            recv(aref(lbrow(z, u)), ("la", u))
        ref = aref(arow(z, 1))
        for dr in range(2):
            send(ref, ref, ("a", dr, 1, 1), zdev[dr])

    def lad_b():
        for u in range(2):
            recv(bref(lbrow(z, u)), ("lb", 0, u, 0))
        own_w.wait()

    def x_cross(c):
        ref = xx.at[NC + c, t]
        recv(ref, ("xc", c))
        for dr in range(2):
            send(ref, ref, ("y", dr, c), ydev[dr])
        send(ref, ref, ("sw", 0, c), other)

    def slice_at(o):
        return (t + 2 * o + NT) % NT

    def x_hop(c, dr):
        ref = xx.at[NC + c, slice_at(-1 if dr == 0 else 1)]
        recv(ref, ("y", dr, c))
        send(ref, ref, ("sw", 1 + dr, c), other)
        if c not in EXTRA and c % 2 == dr:
            send(ref, ref, ("y2", c), ydev[dr])

    def x_far(c):
        ref = xx.at[NC + c, slice_at(2)]
        recv(ref, ("y2", c))
        send(ref, ref, ("sw", 3, c), other)

    def x_swap(c):
        to = 1 - 2 * core
        for k, o in enumerate((0, -1, 1, 2)):
            recv(xx.at[NC + c, (t + to + 2 * o + NT) % NT], ("sw", k, c))

    def mix(m0, half):
        rows = 2 * CH
        for k in range(0, NT, 2):
            a = jnp.concatenate([xx[m0:m0 + 2, k].reshape(rows, KS), xx[m0:m0 + 2, k + 1].reshape(rows, KS)], axis=1)
            p = dot(a, lown[half, k:k + 2].reshape(2 * KS, NM))
            total = p if k == 0 else total + p
        return total.astype(BF)

    def add_output(m0, mixed):
        acc[m0:m0 + 2] -= dot(mixed, rexp[...]).reshape(2, CH, HC)

    def first_mix(m0):
        mixed = mix(m0, 0)
        fm[m0:m0 + 2] = mixed.reshape(2, CH, NM)
        add_output(m0, mixed)

    def partner_mix(p):
        fmo[2 * p:2 * p + 2] = mix(2 * p, 1).reshape(2, CH, NM)
        send(fmo.at[2 * p:2 * p + 2], fm.at[NC + 2 * p:NC + 2 * p + 2], ("fm", p), partner)

    def partner_mix_wait(p):
        recv(fm.at[NC + 2 * p:NC + 2 * p + 2], ("fm", p))

    def partner_output(p):
        add_output(NC + 2 * p, fm[NC + 2 * p:NC + 2 * p + 2].reshape(2 * CH, NM))

    def targets(m_lo, m_n, r_lo, r_n):
        def part(k, carry):
            m0 = m_lo + (k % m_n) * 2
            r = r_lo + k // m_n
            zv = (z + ((r + 1) // 2) * (2 * (r % 2) - 1) + NZ) % NZ
            a = xx[pl.ds(m0, 2), zv].reshape(2 * CH, KS)
            w = wb[pl.ds(pl.multiple_of(zv * KS, KS), KS), :]
            p = dot(a, w).reshape(2, CH, HC)
            if r_lo == 0:
                acc[pl.ds(m0, 2)] = p
            else:
                acc[pl.ds(m0, 2)] += p
            return carry
        lax.fori_loop(0, m_n * r_n, part, 0)

    col_block = iota((NB, HC), 1) // SO

    def expand_right():
        for c in xloads:
            c.wait()
        for j in range(JB):
            rexp[j * NB:(j + 1) * NB] = jnp.where(col_block == j, rh[...], 0).astype(BF)
        pick = (iota((NM, NB), 0) // JB == iota((NM, NB), 1)).astype(BF)
        spread = dot(pick, rh[...])
        rexp2[...] = jnp.where(iota((NM, HC), 0) % JB == iota((NM, HC), 1) // SO, spread, 0.0).astype(BF)

    def gather_left():
        for k in range(1, NT):
            recv(lall.at[(t + NT - k) % NT], ("l", k))
        lall[t] = lpack[t]

    def expand_left():
        def expand(n, carry):
            half, il = n // 8, n % 8
            want = JB * (side + half * (1 - 2 * side))
            row, col = iota((BK, NM), 0), iota((BK, NM), 1)
            choose = jnp.where((row // 8 == il) & (row % 8 == want + col // NB), 1.0, 0.0).astype(BF)
            p = dot(lall[...].reshape(KS, BK), choose)
            row, col = iota((KS, NM), 0), iota((KS, NM), 1)
            keep = col % NB == (row // NB) * 8 + il
            lown[half, :, il] = jnp.where(keep, p, 0.0).astype(BF).reshape(NT, SI, NM)
            return carry
        lax.fori_loop(0, 16, expand, 0)

    events = {"injb": inj_b, "inja": inj_a, "la": lad_a, "lb0": lad_b, "l": gather_left,
              "rex": expand_right, "exp": expand_left}
    at = 0
    while at < len(ORDER):
        name = ORDER[at]
        at += 1
        nums = [int(ch) for ch in name if ch.isdigit()]
        kind = name.rstrip("0123456789")
        if name in events:
            events[name]()
        elif kind == "f":
            first_mix(2 * nums[0])
        elif kind == "t":
            partner_mix(*nums)
        elif kind == "m":
            partner_mix_wait(*nums)
        elif kind == "g":
            partner_output(*nums)
        elif kind in ("o", "x") and name[0:2] != "x2" or kind == "x" and len(nums) == 2:
            r, n = nums[-1], 1
            while r and at < len(ORDER) and ORDER[at] == name[:-1] + str(r + n):
                n, at = n + 1, at + 1
            targets(0 if kind == "o" else NC + 2 * nums[0], 2 if kind == "o" else 1, r, n)
        elif kind == "b":
            b_step(*nums)
        elif kind == "lb":
            lb_wait(*nums)
        elif kind == "a":
            a_step(*nums)
        elif kind == "xc":
            x_cross(*nums)
        elif kind == "y":
            x_hop(*nums)
        elif kind == "e":
            x_far(*nums)
        elif kind == "sw":
            x_swap(*nums)
        else:
            raise ValueError(name)

    gr[...] = jnp.zeros_like(gr)
    lossv[...] = jnp.zeros_like(lossv)

    def right_part(p, carry):
        m0 = 2 * p
        a = acc[pl.ds(m0, 2)].reshape(2 * CH, HC)
        lossv[...] += jnp.sum((a * a).reshape(2 * CH // 8, 8, HC), axis=0)
        sl = (a * (-1.0 / TOKENS)).astype(BF)
        slope[p] = sl
        gr[...] += lax.dot_general(fm[pl.ds(m0, 2)].reshape(2 * CH, NM), sl, TN_DIMS, preferred_element_type=F32)
        return carry
    lax.fori_loop(0, 4, right_part, 0)
    right = jnp.zeros((NB, HC), F32)
    for j in range(JB):
        right += jnp.where(col_block == j, gr[j * NB:(j + 1) * NB], 0.0)
    ggr[:, 0:HC] = right
    ggr[:, HC:RW] = jnp.full((NB, 128), jnp.sum(lossv[...]) / NZ, F32)

    def rows_of(zv):
        return pl.ds(pl.multiple_of(zv * 8, 8), 8)

    def z_send(src, dst, key):
        for k in range(1, NZ):
            send(src.at[rows_of((z + k) % NZ)], dst.at[k], (key, k), dp_dev(x, (z + k) % NZ))

    def z_sum(src, dst, key, out):
        total = src[rows_of(z), :]
        for k in range(1, NZ):
            recv(dst.at[k], (key, k))
            total += dst[k]
        out[...] = total
        return total

    z_send(ggr, zrr, "zr")

    def back_part(p, carry):
        bmt[p] = lax.dot_general(rexp2[...], slope[p], NT_DIMS, preferred_element_type=F32).astype(BF)
        return carry
    lax.fori_loop(0, 4, back_part, 0)

    def left_part(k, carry):
        rows = pl.ds(pl.multiple_of(k * 32, 32), 32)
        total = dot(bmt[0, rows, :], xx[0:2, k].reshape(2 * CH, KS))
        for p in range(1, 4):
            total += dot(bmt[p, rows, :], xx[2 * p:2 * p + 2, k].reshape(2 * CH, KS))
        gl[k] = total
        return carry
    lax.fori_loop(0, NT, left_part, 0)
    row32 = iota((32, 128), 0)
    folded = []
    for k in range(NT):
        v = jnp.zeros((32, 128), F32)
        for p in range(4):
            v += jnp.where(row32 // 8 == p, gl[k, :, p * 128:(p + 1) * 128], 0.0)
        folded.append(jnp.where((row32 // 4) % 2 == 0, v, pltpu.roll(v, 64, 1)))
    ggl[...] = jnp.transpose(jnp.concatenate(folded, axis=0))[0:SI]
    z_send(ggl, zrl, "zl")

    total_r = z_sum(ggr, zrr, "zr", s8r)
    send(s8r, xrr, ("xr",), ladder)
    total_l = z_sum(ggl, zrl, "zl", s8l)
    send(s8l, xrl, ("xl",), ladder)
    recv(xrr, ("xr",))
    full_r = total_r + xrr[...]
    loss_part = full_r[:, HC:RW]
    full_r = full_r[:, 0:HC]
    sq_right = jnp.sum(full_r * full_r)
    recv(xrl, ("xl",))
    full_l = total_l + xrl[...]
    sq_left = jnp.sum(full_l * full_l)
    srow = iota((8, 128), 0)
    tot = jnp.where(srow == 0, sq_right, jnp.where(srow == 1, sq_left, jnp.where(srow == 2, loss_part, 0.0)))
    sc[...] = tot
    for k in range(NZ):
        if k:
            send(sc, scz.at[k], ("sz", k), dp_dev(x, (z + k) % NZ))
        send(sc, scz.at[NZ + k], ("sz", NZ + k), dp_dev(px, (z + k) % NZ))
    s8f[:, 0:HC] = full_r
    s8f[:, HC:HC + NM] = full_l
    send(s8f, xrf, ("xf",), partner)

    def own(v):
        out = v[0:2]
        for k in range(1, NX):
            out = jnp.where(x == k, v[2 * k:2 * k + 2], out)
        return out

    recv(xrf, ("xf",))
    mine, theirs = own(s8f[...]), own(xrf[...])
    rows_a = jnp.where(side == 0, mine, theirs)
    rows_b = jnp.where(side == 0, theirs, mine)
    glr[t] = jnp.zeros((8, 2 * NM), F32)
    glr[t, 0:2, 0:NM] = rows_a[:, HC:HC + NM]
    glr[t, 0:2, NM:2 * NM] = rows_b[:, HC:HC + NM]
    for k in range(1, NT):
        send(glr.at[t], glr.at[t], ("gl", k), t_dev((t + k) % NT))
    for k in range(1, 2 * NZ):
        recv(scz.at[k], ("sz", k))
        tot += scz[k]
    sct[0] = tot
    for k in range(1, NT):
        send(sct.at[0], sct.at[k], ("st", k), t_dev((t + k) % NT))
    lane, col = iota((NM, KS), 0), iota((NM, KS), 1)
    place = jnp.where((lane // JB == 8 * t + col // NB) & (lane % JB == col % JB), 1.0, 0.0)
    for k in range(1, NT):
        recv(glr.at[(t + NT - k) % NT], ("gl", k))
    parts = [glr[k, :, h * NM:(h + 1) * NM] for k in range(NT) for h in range(2)]
    moved = jnp.dot(jnp.concatenate(parts, axis=0), place, precision=lax.Precision.HIGHEST,
                    preferred_element_type=F32)
    mrow, mcol = iota((128, KS), 0), iota((128, KS), 1)
    moved = jnp.where(mrow // 8 == (mcol % NB) // JB, moved, 0.0)
    left_rows = jnp.sum(moved.reshape(16, 8, KS), axis=0)[0:2]
    for k in range(1, NT):
        recv(sct.at[k], ("st", k))
        tot += sct[k]
    scale_right = lax.rsqrt(tot[0:1, 0:1] / (NB * F) + EPS)
    scale_left = lax.rsqrt(tot[1:2, 0:1] / (SI * MID) + EPS)
    dr_out[:, 0:HC] = rows_a[:, 0:HC] * scale_right
    dr_out[:, HC:2 * HC] = rows_b[:, 0:HC] * scale_right
    dl_out[...] = left_rows * scale_left
    loss_out[...] = tot[2:3, :] / (2.0 * TOKENS)
    for copy in sends:
        copy.wait_send()


def local(tokens, dense_weight, left_factor, right_factor):
    vmem = pl.BlockSpec(memory_space=pltpu.VMEM)
    hbm = pl.BlockSpec(memory_space=pl.ANY)
    dir_left, dir_right, loss = pl.pallas_call(
        kernel,
        out_shape=(jax.ShapeDtypeStruct((2, KS), F32),
                   jax.ShapeDtypeStruct((2, 2 * HC), F32),
                   jax.ShapeDtypeStruct((1, 128), F32)),
        in_specs=[hbm] * 4,
        out_specs=(vmem,) * 3,
        scratch_shapes=[
            pltpu.VMEM((2 * NC, NT, CH, KS), BF),
            pltpu.VMEM((4096, HC), BF),
            pltpu.VMEM((SI, KS), BF),
            pltpu.VMEM((NT, SI, BK), BF),
            pltpu.VMEM((NT, SI, BK), BF),
            pltpu.VMEM((2, NT, 8, SI, NM), BF),
            pltpu.VMEM((NB, HC), BF),
            pltpu.VMEM((NM, HC), BF),
            pltpu.VMEM((NM, HC), BF),
            pltpu.VMEM((2 * NC, CH, NM), BF),
            pltpu.VMEM((NC, CH, NM), BF),
            pltpu.VMEM((2 * NC, CH, HC), F32),
            pltpu.VMEM((NC, 2 * CH, HC), BF),
            pltpu.VMEM((NC, NM, 2 * CH), BF),
            pltpu.VMEM((NM, HC), F32),
            pltpu.VMEM((NT, 32, KS), F32),
            pltpu.VMEM((8, HC), F32),
            pltpu.VMEM((NB, RW), F32),
            pltpu.VMEM((NB, NM), F32),
            pltpu.VMEM((NZ, 8, RW), F32),
            pltpu.VMEM((NZ, 8, NM), F32),
            pltpu.VMEM((8, RW), F32),
            pltpu.VMEM((8, NM), F32),
            pltpu.VMEM((8, RW), F32),
            pltpu.VMEM((8, NM), F32),
            pltpu.VMEM((8, HC + NM), F32),
            pltpu.VMEM((8, HC + NM), F32),
            pltpu.VMEM((8, 128), F32),
            pltpu.VMEM((2 * NZ, 8, 128), F32),
            pltpu.VMEM((NT, 8, 128), F32),
            pltpu.VMEM((NT, 8, 2 * NM), F32),
            pltpu.SemaphoreType.DMA((176,)),
            pltpu.SemaphoreType.DMA((176,)),
            pltpu.SemaphoreType.DMA((16,)),
        ],
        compiler_params=pltpu.CompilerParams(
            collective_id=0, has_side_effects=True, vmem_limit_bytes=60 * 1024 * 1024),
    )(tokens.reshape(NC, CH, 4096), dense_weight, left_factor, right_factor)
    return (dir_left, dir_right, loss[0, 0])


def solution(mesh):
    in_specs = (P("dp", None), P("dp", "tensor"), P(None, "tensor"), P(None, "tensor"))
    out_specs = (P("dp", "tensor"), P("dp", "tensor"), P())
    return jax.shard_map(local, mesh=mesh, in_specs=in_specs, out_specs=out_specs, check_vma=False)
```

```python
import jax
import jax.numpy as jnp
from jax import lax
from jax.experimental import pallas as pl
from jax.experimental.pallas import tpu as pltpu
from jax.sharding import PartitionSpec as P

MESH = pl.DeviceIdType.MESH
F = 14336
NB = 64
SI = 64
SO = 224
MID = 4096
TOKENS = 30720
EPS = 1e-06

NX, NZ, NT = 4, 8, 8
CH = 240
NC = 4
KS = 512
HC = 896
NA = 384
BK = 128
JB = 4
NM = JB * NB
RW = HC + 128
BF = jnp.bfloat16
F32 = jnp.float32
NT_DIMS = (((1,), (1,)), ((), ()))
TN_DIMS = (((0,), (0,)), ((), ()))
EXTRA = (2, 3)
ORDER = (
    "rex", "l", "exp", "injb", "b010", "b011", "t0", "inja", "t1", "b110", "b111", "lb0", "xc0", "b020",
    "b021", "lb010", "a010", "a011", "lb011", "xc1", "la", "b120", "b121", "o0", "y00", "y01", "f0", "b030",
    "b031", "lb110", "xc2", "f1", "y10", "y11", "a020", "a021", "lb111", "lb020", "xc3", "lb021", "a110",
    "a111", "o1", "e0", "y21", "o2", "b130", "b131", "lb120", "sw0", "e2", "lb121", "b040", "y20", "e1",
    "a031", "sw2", "sw1", "x00", "x01", "lb030", "x02", "e3", "a030", "y30", "y31", "lb031", "a121", "o3",
    "sw3", "x10", "x11", "a120", "b141", "lb130", "m0", "x12", "x03", "x13", "o4", "lb131", "x04", "a131",
    "a040", "x14", "lb040", "m1", "o5", "x05", "x15", "lb141", "a130", "o6", "x06", "a141", "x16", "o7",
    "x07", "x17", "g0", "g1")


def dot(a, b):
    return jnp.dot(a, b, preferred_element_type=F32)


def iota(shape, axis):
    return lax.broadcasted_iota(jnp.int32, shape, axis)


def kernel(x_hbm, w_hbm, l_hbm, r_hbm, dl_out, dr_out, loss_out,
           xx, wb, lraw, lpack, lall, lown, rh, rexp, rexp2, fm, fmo, acc, slope, bmt,
           gr, gl, lossv, ggr, ggl, zrr, zrl, s8r, s8l, xrr, xrl, s8f, xrf, sc, scz, sct, glr, ssem, rsem, lsem):
    d = lax.axis_index("dp")
    t = lax.axis_index("tensor")
    x, z = d % NX, d // NX
    y, core = t // 2, t % 2
    side = ((x + 1) // 2) % 2
    q = x // 2

    def dp_dev(xv, zv):
        return {"dp": zv * NX + xv, "tensor": t}

    def t_dev(tv):
        return {"dp": d, "tensor": tv}

    partner = dp_dev(x + 1 - 2 * (x % 2), z)
    ladder = dp_dev(3 - x, z)
    zdev = (dp_dev(x, (z + 1) % NZ), dp_dev(x, (z + NZ - 1) % NZ))
    ydev = (t_dev((t + 2) % NT), t_dev((t + NT - 2) % NT))
    other = t_dev(t + 1 - 2 * core)

    ids, sends = {}, []

    def rid(key):
        return ids.setdefault(key, len(ids))

    def send(src, dst, key, dev):
        copy = pltpu.make_async_remote_copy(
            src_ref=src, dst_ref=dst, send_sem=ssem.at[len(sends)], recv_sem=rsem.at[rid(key)],
            device_id=dev, device_id_type=MESH)
        copy.start()
        sends.append(copy)

    def recv(ref, key):
        pltpu.make_async_remote_copy(
            src_ref=ref, dst_ref=ref, send_sem=ssem.at[0], recv_sem=rsem.at[rid(key)],
            device_id=ladder, device_id_type=MESH).wait_recv()

    loads = [pltpu.make_async_copy(l_hbm, lraw, lsem.at[0]),
             pltpu.make_async_copy(r_hbm.at[:, pl.ds(pl.multiple_of(side * HC, 128), HC)], rh, lsem.at[1])]
    own_rows = pl.ds(pl.multiple_of(z * KS + x * BK, BK), BK)
    own_w = pltpu.make_async_copy(
        w_hbm.at[:, pl.ds(pl.multiple_of(side * HC, 128), HC)], wb.at[own_rows, :], lsem.at[2])
    own_w.start()
    for c in loads:
        c.start()
    xloads = []
    for k in range(NT):
        c = pltpu.make_async_copy(x_hbm.at[:, :, pl.ds(k * KS, KS)], xx.at[0:NC, k], lsem.at[3 + k])
        c.start()
        xloads.append(c)

    barrier = pltpu.get_barrier_semaphore()
    px = x + 1 - 2 * (x % 2)
    peers = ([ladder] + [dp_dev(px, (z + k) % NZ) for k in range(NZ)]
             + [dp_dev(x, (z + k) % NZ) for k in range(1, NZ)]
             + [t_dev((t + k) % NT) for k in range(1, NT)])
    for dev in peers:
        pl.semaphore_signal(barrier, inc=1, device_id=dev, device_id_type=MESH)
    for c in loads:
        c.wait()
    lrow, lcol = iota((KS, BK), 0), iota((KS, BK), 1)
    for k in range(NT):
        take = jnp.where((lcol < 64) & (lrow // NB == lcol // 8) & (lrow % NB == 8 * k + lcol % 8), 1.0, 0.0)
        lpack[k] = dot(lraw[...], take.astype(BF)).astype(BF)
    pl.semaphore_wait(barrier, len(peers))

    def brow(zv, u):
        r = x % 2 if u == 0 else 1 - x % 2
        return pl.ds(pl.multiple_of(zv * KS + q * 256 + r * BK, BK), BK)

    def lbrow(zv, u):
        r = x % 2 if u == 0 else 1 - x % 2
        return pl.ds(pl.multiple_of(zv * KS + (1 - q) * 256 + (1 - r) * BK, BK), BK)

    def arow(zv, v):
        qq = q if v == 0 else 1 - q
        return pl.ds(pl.multiple_of(zv * KS + qq * 256, 256), 256)

    def bref(rows):
        return wb.at[rows, NA:HC]

    def aref(rows):
        return wb.at[rows, 0:NA]

    def zat(o):
        return (z + o + NZ) % NZ

    def hops(direction, first):
        return 4 if direction == (0 if first else 1) else 3

    bcol = pl.ds(pl.multiple_of(side * HC + NA, 128), HC - NA)
    acol = pl.ds(pl.multiple_of(side * HC, 128), NA)
    obcol = pl.ds(pl.multiple_of((1 - side) * HC + NA, 128), HC - NA)
    oacol = pl.ds(pl.multiple_of((1 - side) * HC, 128), NA)

    send(w_hbm.at[:, obcol], bref(own_rows), ("injb",), partner)
    for k in range(1, NT):
        send(lpack.at[(t + k) % NT], lall.at[t], ("l", k), t_dev((t + k) % NT))
    for dr in range(2):
        send(w_hbm.at[:, bcol], bref(own_rows), ("b", dr, 0, 1), zdev[dr])
    send(w_hbm.at[:, bcol], bref(own_rows), ("lb", 0, 0, 0), ladder)
    send(w_hbm.at[:, oacol], aref(own_rows), ("inja",), partner)
    send(w_hbm.at[:, acol], aref(own_rows), ("la", 0), ladder)
    for dr in range(2):
        send(w_hbm.at[:, acol], aref(own_rows), ("a0", dr, 0), zdev[dr])
    for c in range(NC):
        send(x_hbm.at[c, :, pl.ds(pl.multiple_of(t * KS, KS), KS)], xx.at[NC + c, t], ("xc", c), partner)
    far = (t + 4) % NT
    for c in EXTRA:
        send(x_hbm.at[c, :, pl.ds(pl.multiple_of(far * KS, KS), KS)], xx.at[NC + c, far], ("y2", c), partner)

    def zfrom(dr, s):
        return zat(-s if dr == 0 else s)

    def b_step(u, s, dr):
        ref = bref(brow(zfrom(dr, s), u))
        recv(ref, ("b", dr, u, s))
        if s < hops(dr, u == 0):
            send(ref, ref, ("b", dr, u, s + 1), zdev[dr])
        send(ref, ref, ("lb", dr, u, s), ladder)

    def lb_wait(u, s, dr):
        recv(bref(lbrow(zfrom(dr, s), u)), ("lb", dr, u, s))

    def a_step(v, s, dr):
        zv = zfrom(dr, s)
        ref = aref(arow(zv, v))
        if v == 0 and s == 1:
            for u in range(2):
                recv(aref(brow(zv, u)), ("a0", dr, u))
        else:
            recv(ref, ("a", dr, v, s))
        if s < hops(dr, v == 0):
            send(ref, ref, ("a", dr, v, s + 1), zdev[dr])

    def inj_b():
        ref = bref(brow(z, 1))
        recv(ref, ("injb",))
        for dr in range(2):
            send(ref, ref, ("b", dr, 1, 1), zdev[dr])
        send(ref, ref, ("lb", 0, 1, 0), ladder)

    def inj_a():
        ref = aref(brow(z, 1))
        recv(ref, ("inja",))
        send(ref, ref, ("la", 1), ladder)
        for dr in range(2):
            send(ref, ref, ("a0", dr, 1), zdev[dr])

    def lad_a():
        for u in range(2):
            recv(aref(lbrow(z, u)), ("la", u))
        ref = aref(arow(z, 1))
        for dr in range(2):
            send(ref, ref, ("a", dr, 1, 1), zdev[dr])

    def lad_b():
        for u in range(2):
            recv(bref(lbrow(z, u)), ("lb", 0, u, 0))
        own_w.wait()

    def x_cross(c):
        ref = xx.at[NC + c, t]
        recv(ref, ("xc", c))
        for dr in range(2):
            send(ref, ref, ("y", dr, c), ydev[dr])
        send(ref, ref, ("sw", 0, c), other)

    def slice_at(o):
        return (t + 2 * o + NT) % NT

    def x_hop(c, dr):
        ref = xx.at[NC + c, slice_at(-1 if dr == 0 else 1)]
        recv(ref, ("y", dr, c))
        send(ref, ref, ("sw", 1 + dr, c), other)
        if c not in EXTRA and c % 2 == dr:
            send(ref, ref, ("y2", c), ydev[dr])

    def x_far(c):
        ref = xx.at[NC + c, slice_at(2)]
        recv(ref, ("y2", c))
        send(ref, ref, ("sw", 3, c), other)

    def x_swap(c):
        to = 1 - 2 * core
        for k, o in enumerate((0, -1, 1, 2)):
            recv(xx.at[NC + c, (t + to + 2 * o + NT) % NT], ("sw", k, c))

    def mix(m0, half):
        rows = 2 * CH
        for k in range(0, NT, 2):
            a = jnp.concatenate([xx[m0:m0 + 2, k].reshape(rows, KS), xx[m0:m0 + 2, k + 1].reshape(rows, KS)], axis=1)
            p = dot(a, lown[half, k:k + 2].reshape(2 * KS, NM))
            total = p if k == 0 else total + p
        return total.astype(BF)

    def add_output(m0, mixed):
        acc[m0:m0 + 2] -= dot(mixed, rexp[...]).reshape(2, CH, HC)

    def first_mix(m0):
        mixed = mix(m0, 0)
        fm[m0:m0 + 2] = mixed.reshape(2, CH, NM)
        add_output(m0, mixed)

    def partner_mix(p):
        fmo[2 * p:2 * p + 2] = mix(2 * p, 1).reshape(2, CH, NM)
        send(fmo.at[2 * p:2 * p + 2], fm.at[NC + 2 * p:NC + 2 * p + 2], ("fm", p), partner)

    def partner_mix_wait(p):
        recv(fm.at[NC + 2 * p:NC + 2 * p + 2], ("fm", p))

    def partner_output(p):
        add_output(NC + 2 * p, fm[NC + 2 * p:NC + 2 * p + 2].reshape(2 * CH, NM))

    def targets(m_lo, m_n, r_lo, r_n):
        def part(k, carry):
            m0 = m_lo + (k % m_n) * 2
            r = r_lo + k // m_n
            zv = (z + ((r + 1) // 2) * (2 * (r % 2) - 1) + NZ) % NZ
            a = xx[pl.ds(m0, 2), zv].reshape(2 * CH, KS)
            w = wb[pl.ds(pl.multiple_of(zv * KS, KS), KS), :]
            p = dot(a, w).reshape(2, CH, HC)
            if r_lo == 0:
                acc[pl.ds(m0, 2)] = p
            else:
                acc[pl.ds(m0, 2)] += p
            return carry
        lax.fori_loop(0, m_n * r_n, part, 0)

    col_block = iota((NB, HC), 1) // SO

    def expand_right():
        for c in xloads:
            c.wait()
        for j in range(JB):
            rexp[j * NB:(j + 1) * NB] = jnp.where(col_block == j, rh[...], 0).astype(BF)
        pick = (iota((NM, NB), 0) // JB == iota((NM, NB), 1)).astype(BF)
        spread = dot(pick, rh[...])
        rexp2[...] = jnp.where(iota((NM, HC), 0) % JB == iota((NM, HC), 1) // SO, spread, 0.0).astype(BF)

    def gather_left():
        for k in range(1, NT):
            recv(lall.at[(t + NT - k) % NT], ("l", k))
        lall[t] = lpack[t]

    def expand_left():
        def expand(n, carry):
            half, il = n // 8, n % 8
            want = JB * (side + half * (1 - 2 * side))
            row, col = iota((BK, NM), 0), iota((BK, NM), 1)
            choose = jnp.where((row // 8 == il) & (row % 8 == want + col // NB), 1.0, 0.0).astype(BF)
            p = dot(lall[...].reshape(KS, BK), choose)
            row, col = iota((KS, NM), 0), iota((KS, NM), 1)
            keep = col % NB == (row // NB) * 8 + il
            lown[half, :, il] = jnp.where(keep, p, 0.0).astype(BF).reshape(NT, SI, NM)
            return carry
        lax.fori_loop(0, 16, expand, 0)

    events = {"injb": inj_b, "inja": inj_a, "la": lad_a, "lb0": lad_b, "l": gather_left,
              "rex": expand_right, "exp": expand_left}
    at = 0
    while at < len(ORDER):
        name = ORDER[at]
        at += 1
        nums = [int(ch) for ch in name if ch.isdigit()]
        kind = name.rstrip("0123456789")
        if name in events:
            events[name]()
        elif kind == "f":
            first_mix(2 * nums[0])
        elif kind == "t":
            partner_mix(*nums)
        elif kind == "m":
            partner_mix_wait(*nums)
        elif kind == "g":
            partner_output(*nums)
        elif kind in ("o", "x") and name[0:2] != "x2" or kind == "x" and len(nums) == 2:
            r, n = nums[-1], 1
            while r and at < len(ORDER) and ORDER[at] == name[:-1] + str(r + n):
                n, at = n + 1, at + 1
            targets(0 if kind == "o" else NC + 2 * nums[0], 2 if kind == "o" else 1, r, n)
        elif kind == "b":
            b_step(*nums)
        elif kind == "lb":
            lb_wait(*nums)
        elif kind == "a":
            a_step(*nums)
        elif kind == "xc":
            x_cross(*nums)
        elif kind == "y":
            x_hop(*nums)
        elif kind == "e":
            x_far(*nums)
        elif kind == "sw":
            x_swap(*nums)
        else:
            raise ValueError(name)

    gr[...] = jnp.zeros_like(gr)
    lossv[...] = jnp.zeros_like(lossv)

    def right_part(p, carry):
        m0 = 2 * p
        a = acc[pl.ds(m0, 2)].reshape(2 * CH, HC)
        lossv[...] += jnp.sum((a * a).reshape(2 * CH // 8, 8, HC), axis=0)
        sl = (a * (-1.0 / TOKENS)).astype(BF)
        slope[p] = sl
        gr[...] += lax.dot_general(fm[pl.ds(m0, 2)].reshape(2 * CH, NM), sl, TN_DIMS, preferred_element_type=F32)
        return carry
    lax.fori_loop(0, 4, right_part, 0)
    right = jnp.zeros((NB, HC), F32)
    for j in range(JB):
        right += jnp.where(col_block == j, gr[j * NB:(j + 1) * NB], 0.0)
    ggr[...] = right
    s8r[:, HC:RW] = jnp.full((8, 128), jnp.sum(lossv[...]), F32)

    def rows_of(zv):
        return pl.ds(pl.multiple_of(zv * 8, 8), 8)

    def z_send(src, dst, key):
        for k in (4, 3, 5, 2, 6, 1, 7):
            send(src.at[rows_of((z + k) % NZ)], dst.at[k], (key, k), dp_dev(x, (z + k) % NZ))

    def z_sum(src, dst, key, out):
        total = src[rows_of(z), :]
        for k in range(1, NZ):
            recv(dst.at[k], (key, k))
            total += dst[k]
        out[:, 0:total.shape[1]] = total
        return total

    z_send(ggr, zrr, "zr")

    def back_part(p, carry):
        bmt[p] = lax.dot_general(rexp2[...], slope[p], NT_DIMS, preferred_element_type=F32).astype(BF)
        return carry
    lax.fori_loop(0, 4, back_part, 0)

    def left_part(k, carry):
        rows = pl.ds(pl.multiple_of(k * 32, 32), 32)
        total = dot(bmt[0, rows, :], xx[0:2, k].reshape(2 * CH, KS))
        for p in range(1, 4):
            total += dot(bmt[p, rows, :], xx[2 * p:2 * p + 2, k].reshape(2 * CH, KS))
        gl[k] = total
        return carry
    lax.fori_loop(0, NT, left_part, 0)
    row32 = iota((32, 128), 0)
    folded = []
    for k in range(NT):
        v = jnp.zeros((32, 128), F32)
        for p in range(4):
            v += jnp.where(row32 // 8 == p, gl[k, :, p * 128:(p + 1) * 128], 0.0)
        folded.append(jnp.where((row32 // 4) % 2 == 0, v, pltpu.roll(v, 64, 1)))
    ggl[...] = jnp.transpose(jnp.concatenate(folded, axis=0))[0:SI]
    z_send(ggl, zrl, "zl")

    total_r = z_sum(ggr, zrr, "zr", s8r)
    send(s8r, xrr, ("xr",), ladder)
    total_l = z_sum(ggl, zrl, "zl", s8l)
    send(s8l, xrl, ("xl",), ladder)
    recv(xrr, ("xr",))
    full_r = total_r + xrr[:, 0:HC]
    loss_part = s8r[:, HC:RW] + xrr[:, HC:RW]
    sq_right = jnp.sum(full_r * full_r)
    recv(xrl, ("xl",))
    full_l = total_l + xrl[...]
    sq_left = jnp.sum(full_l * full_l)
    srow = iota((8, 128), 0)
    tot = jnp.where(srow == 0, sq_right, jnp.where(srow == 1, sq_left, jnp.where(srow == 2, loss_part, 0.0)))
    sc[...] = tot
    for k in (4, 3, 5, 2, 6, 1, 7, 0):
        if k:
            send(sc, scz.at[k], ("sz", k), dp_dev(x, (z + k) % NZ))
        send(sc, scz.at[NZ + k], ("sz", NZ + k), dp_dev(px, (z + k) % NZ))
    s8f[:, 0:HC] = full_r
    s8f[:, HC:HC + NM] = full_l
    send(s8f, xrf, ("xf",), partner)

    def own(v):
        out = v[0:2]
        for k in range(1, NX):
            out = jnp.where(x == k, v[2 * k:2 * k + 2], out)
        return out

    recv(xrf, ("xf",))
    mine, theirs = own(s8f[...]), own(xrf[...])
    rows_a = jnp.where(side == 0, mine, theirs)
    rows_b = jnp.where(side == 0, theirs, mine)
    glr[t] = jnp.zeros((8, 2 * NM), F32)
    glr[t, 0:2, 0:NM] = rows_a[:, HC:HC + NM]
    glr[t, 0:2, NM:2 * NM] = rows_b[:, HC:HC + NM]
    for k in range(1, NT):
        send(glr.at[t], glr.at[t], ("gl", k), t_dev((t + k) % NT))
    for k in range(1, 2 * NZ):
        recv(scz.at[k], ("sz", k))
        tot += scz[k]
    sct[0] = tot
    for k in range(1, NT):
        send(sct.at[0], sct.at[k], ("st", k), t_dev((t + k) % NT))
    lane, col = iota((NM, KS), 0), iota((NM, KS), 1)
    place = jnp.where((lane // JB == 8 * t + col // NB) & (lane % JB == col % JB), 1.0, 0.0)
    for k in range(1, NT):
        recv(glr.at[(t + NT - k) % NT], ("gl", k))
    parts = [glr[k, :, h * NM:(h + 1) * NM] for k in range(NT) for h in range(2)]
    moved = jnp.dot(jnp.concatenate(parts, axis=0), place, precision=lax.Precision.HIGHEST,
                    preferred_element_type=F32)
    mrow, mcol = iota((128, KS), 0), iota((128, KS), 1)
    moved = jnp.where(mrow // 8 == (mcol % NB) // JB, moved, 0.0)
    left_rows = jnp.sum(moved.reshape(16, 8, KS), axis=0)[0:2]
    for k in range(1, NT):
        recv(sct.at[k], ("st", k))
        tot += sct[k]
    scale_right = lax.rsqrt(tot[0:1, 0:1] / (NB * F) + EPS)
    scale_left = lax.rsqrt(tot[1:2, 0:1] / (SI * MID) + EPS)
    dr_out[:, 0:HC] = rows_a[:, 0:HC] * scale_right
    dr_out[:, HC:2 * HC] = rows_b[:, 0:HC] * scale_right
    dl_out[...] = left_rows * scale_left
    loss_out[...] = tot[2:3, :] / (2.0 * TOKENS)
    for copy in sends:
        copy.wait_send()


def local(tokens, dense_weight, left_factor, right_factor):
    vmem = pl.BlockSpec(memory_space=pltpu.VMEM)
    hbm = pl.BlockSpec(memory_space=pl.ANY)
    dir_left, dir_right, loss = pl.pallas_call(
        kernel,
        out_shape=(jax.ShapeDtypeStruct((2, KS), F32),
                   jax.ShapeDtypeStruct((2, 2 * HC), F32),
                   jax.ShapeDtypeStruct((1, 128), F32)),
        in_specs=[hbm] * 4,
        out_specs=(vmem,) * 3,
        scratch_shapes=[
            pltpu.VMEM((2 * NC, NT, CH, KS), BF),
            pltpu.VMEM((4096, HC), BF),
            pltpu.VMEM((SI, KS), BF),
            pltpu.VMEM((NT, SI, BK), BF),
            pltpu.VMEM((NT, SI, BK), BF),
            pltpu.VMEM((2, NT, 8, SI, NM), BF),
            pltpu.VMEM((NB, HC), BF),
            pltpu.VMEM((NM, HC), BF),
            pltpu.VMEM((NM, HC), BF),
            pltpu.VMEM((2 * NC, CH, NM), BF),
            pltpu.VMEM((NC, CH, NM), BF),
            pltpu.VMEM((2 * NC, CH, HC), F32),
            pltpu.VMEM((NC, 2 * CH, HC), BF),
            pltpu.VMEM((NC, NM, 2 * CH), BF),
            pltpu.VMEM((NM, HC), F32),
            pltpu.VMEM((NT, 32, KS), F32),
            pltpu.VMEM((8, HC), F32),
            pltpu.VMEM((NB, HC), F32),
            pltpu.VMEM((NB, NM), F32),
            pltpu.VMEM((NZ, 8, HC), F32),
            pltpu.VMEM((NZ, 8, NM), F32),
            pltpu.VMEM((8, RW), F32),
            pltpu.VMEM((8, NM), F32),
            pltpu.VMEM((8, RW), F32),
            pltpu.VMEM((8, NM), F32),
            pltpu.VMEM((8, HC + NM), F32),
            pltpu.VMEM((8, HC + NM), F32),
            pltpu.VMEM((8, 128), F32),
            pltpu.VMEM((2 * NZ, 8, 128), F32),
            pltpu.VMEM((NT, 8, 128), F32),
            pltpu.VMEM((NT, 8, 2 * NM), F32),
            pltpu.SemaphoreType.DMA((176,)),
            pltpu.SemaphoreType.DMA((176,)),
            pltpu.SemaphoreType.DMA((16,)),
        ],
        compiler_params=pltpu.CompilerParams(
            collective_id=0, has_side_effects=True, vmem_limit_bytes=60 * 1024 * 1024),
    )(tokens.reshape(NC, CH, 4096), dense_weight, left_factor, right_factor)
    return (dir_left, dir_right, loss[0, 0])


def solution(mesh):
    in_specs = (P("dp", None), P("dp", "tensor"), P(None, "tensor"), P(None, "tensor"))
    out_specs = (P("dp", "tensor"), P("dp", "tensor"), P())
    return jax.shard_map(local, mesh=mesh, in_specs=in_specs, out_specs=out_specs, check_vma=False)
```

```python
import jax
import jax.numpy as jnp
from jax import lax
from jax.experimental import pallas as pl
from jax.experimental.pallas import tpu as pltpu
from jax.sharding import PartitionSpec as P

MESH = pl.DeviceIdType.MESH
F = 14336
NB = 64
SI = 64
SO = 224
MID = 4096
TOKENS = 30720
EPS = 1e-06

NX, NZ, NT = 4, 8, 8
CH = 240
NC = 4
KS = 512
HC = 896
NA = 384
BK = 128
JB = 4
NM = JB * NB
RW = HC + 128
BF = jnp.bfloat16
F32 = jnp.float32
NT_DIMS = (((1,), (1,)), ((), ()))
TN_DIMS = (((0,), (0,)), ((), ()))
EXTRA = (2, 3)
ORDER = (
    "rex", "l", "exp", "injb", "b010", "b011", "t0", "inja", "t1", "b110", "b111", "lb0", "xc0", "b020",
    "b021", "lb010", "a010", "a011", "lb011", "xc1", "la", "b120", "b121", "o0", "y00", "y01", "f0", "b030",
    "b031", "lb110", "xc2", "f1", "y10", "y11", "a020", "a021", "lb111", "lb020", "xc3", "lb021", "a110",
    "a111", "o1", "e0", "y21", "o2", "b130", "b131", "lb120", "sw0", "e2", "lb121", "b040", "y20", "e1",
    "a031", "sw2", "sw1", "x00", "x01", "lb030", "x02", "e3", "a030", "y30", "y31", "lb031", "a121", "o3",
    "sw3", "x10", "x11", "a120", "b141", "lb130", "m0", "x12", "x03", "x13", "o4", "lb131", "x04", "a131",
    "a040", "x14", "lb040", "m1", "o5", "x05", "x15", "lb141", "a130", "o6", "x06", "a141", "x16", "o7",
    "x07", "x17", "g0", "g1")


def dot(a, b):
    return jnp.dot(a, b, preferred_element_type=F32)


def iota(shape, axis):
    return lax.broadcasted_iota(jnp.int32, shape, axis)


def kernel(x_hbm, w_hbm, l_hbm, r_hbm, dl_out, dr_out, loss_out,
           xx, wb, lraw, lpack, lall, lown, rh, rexp, rexp2, fm, fmo, acc, slope, bmt,
           gr, gl, lossv, ggr, ggl, zrr, zrl, s8r, s8l, xrr, xrl, s8f, xrf, sc, scz, sct, glr, ssem, rsem, lsem):
    d = lax.axis_index("dp")
    t = lax.axis_index("tensor")
    x, z = d % NX, d // NX
    y, core = t // 2, t % 2
    side = ((x + 1) // 2) % 2
    q = x // 2

    def dp_dev(xv, zv):
        return {"dp": zv * NX + xv, "tensor": t}

    def t_dev(tv):
        return {"dp": d, "tensor": tv}

    partner = dp_dev(x + 1 - 2 * (x % 2), z)
    ladder = dp_dev(3 - x, z)
    zdev = (dp_dev(x, (z + 1) % NZ), dp_dev(x, (z + NZ - 1) % NZ))
    ydev = (t_dev((t + 2) % NT), t_dev((t + NT - 2) % NT))
    other = t_dev(t + 1 - 2 * core)

    ids, sends = {}, []

    def rid(key):
        return ids.setdefault(key, len(ids))

    def send(src, dst, key, dev):
        copy = pltpu.make_async_remote_copy(
            src_ref=src, dst_ref=dst, send_sem=ssem.at[len(sends)], recv_sem=rsem.at[rid(key)],
            device_id=dev, device_id_type=MESH)
        copy.start()
        sends.append(copy)

    def recv(ref, key):
        pltpu.make_async_remote_copy(
            src_ref=ref, dst_ref=ref, send_sem=ssem.at[0], recv_sem=rsem.at[rid(key)],
            device_id=ladder, device_id_type=MESH).wait_recv()

    loads = [pltpu.make_async_copy(l_hbm, lraw, lsem.at[0]),
             pltpu.make_async_copy(r_hbm.at[:, pl.ds(pl.multiple_of(side * HC, 128), HC)], rh, lsem.at[1])]
    own_rows = pl.ds(pl.multiple_of(z * KS + x * BK, BK), BK)
    own_w = pltpu.make_async_copy(
        w_hbm.at[:, pl.ds(pl.multiple_of(side * HC, 128), HC)], wb.at[own_rows, :], lsem.at[2])
    own_w.start()
    for c in loads:
        c.start()
    xloads = []
    for k in range(NT):
        c = pltpu.make_async_copy(x_hbm.at[:, :, pl.ds(k * KS, KS)], xx.at[0:NC, k], lsem.at[3 + k])
        c.start()
        xloads.append(c)

    barrier = pltpu.get_barrier_semaphore()
    px = x + 1 - 2 * (x % 2)
    peers = ([ladder] + [dp_dev(px, (z + k) % NZ) for k in range(NZ)]
             + [dp_dev(x, (z + k) % NZ) for k in range(1, NZ)]
             + [t_dev((t + k) % NT) for k in range(1, NT)])
    for dev in peers:
        pl.semaphore_signal(barrier, inc=1, device_id=dev, device_id_type=MESH)
    for c in loads:
        c.wait()
    lrow, lcol = iota((KS, BK), 0), iota((KS, BK), 1)
    for k in range(NT):
        take = jnp.where((lcol < 64) & (lrow // NB == lcol // 8) & (lrow % NB == 8 * k + lcol % 8), 1.0, 0.0)
        lpack[k] = dot(lraw[...], take.astype(BF)).astype(BF)
    pl.semaphore_wait(barrier, len(peers))

    def brow(zv, u):
        r = x % 2 if u == 0 else 1 - x % 2
        return pl.ds(pl.multiple_of(zv * KS + q * 256 + r * BK, BK), BK)

    def lbrow(zv, u):
        r = x % 2 if u == 0 else 1 - x % 2
        return pl.ds(pl.multiple_of(zv * KS + (1 - q) * 256 + (1 - r) * BK, BK), BK)

    def arow(zv, v):
        qq = q if v == 0 else 1 - q
        return pl.ds(pl.multiple_of(zv * KS + qq * 256, 256), 256)

    def bref(rows):
        return wb.at[rows, NA:HC]

    def aref(rows):
        return wb.at[rows, 0:NA]

    def zat(o):
        return (z + o + NZ) % NZ

    def hops(direction, first):
        return 4 if direction == (0 if first else 1) else 3

    bcol = pl.ds(pl.multiple_of(side * HC + NA, 128), HC - NA)
    acol = pl.ds(pl.multiple_of(side * HC, 128), NA)
    obcol = pl.ds(pl.multiple_of((1 - side) * HC + NA, 128), HC - NA)
    oacol = pl.ds(pl.multiple_of((1 - side) * HC, 128), NA)

    send(w_hbm.at[:, obcol], bref(own_rows), ("injb",), partner)
    for k in range(1, NT):
        send(lpack.at[(t + k) % NT], lall.at[t], ("l", k), t_dev((t + k) % NT))
    for dr in range(2):
        send(w_hbm.at[:, bcol], bref(own_rows), ("b", dr, 0, 1), zdev[dr])
    send(w_hbm.at[:, bcol], bref(own_rows), ("lb", 0, 0, 0), ladder)
    send(w_hbm.at[:, oacol], aref(own_rows), ("inja",), partner)
    send(w_hbm.at[:, acol], aref(own_rows), ("la", 0), ladder)
    for dr in range(2):
        send(w_hbm.at[:, acol], aref(own_rows), ("a0", dr, 0), zdev[dr])
    for c in range(NC):
        send(x_hbm.at[c, :, pl.ds(pl.multiple_of(t * KS, KS), KS)], xx.at[NC + c, t], ("xc", c), partner)
    far = (t + 4) % NT
    for c in EXTRA:
        send(x_hbm.at[c, :, pl.ds(pl.multiple_of(far * KS, KS), KS)], xx.at[NC + c, far], ("y2", c), partner)

    def zfrom(dr, s):
        return zat(-s if dr == 0 else s)

    def b_step(u, s, dr):
        ref = bref(brow(zfrom(dr, s), u))
        recv(ref, ("b", dr, u, s))
        if s < hops(dr, u == 0):
            send(ref, ref, ("b", dr, u, s + 1), zdev[dr])
        send(ref, ref, ("lb", dr, u, s), ladder)

    def lb_wait(u, s, dr):
        recv(bref(lbrow(zfrom(dr, s), u)), ("lb", dr, u, s))

    def a_step(v, s, dr):
        zv = zfrom(dr, s)
        ref = aref(arow(zv, v))
        if v == 0 and s == 1:
            for u in range(2):
                recv(aref(brow(zv, u)), ("a0", dr, u))
        else:
            recv(ref, ("a", dr, v, s))
        if s < hops(dr, v == 0):
            send(ref, ref, ("a", dr, v, s + 1), zdev[dr])

    def inj_b():
        ref = bref(brow(z, 1))
        recv(ref, ("injb",))
        for dr in range(2):
            send(ref, ref, ("b", dr, 1, 1), zdev[dr])
        send(ref, ref, ("lb", 0, 1, 0), ladder)

    def inj_a():
        ref = aref(brow(z, 1))
        recv(ref, ("inja",))
        send(ref, ref, ("la", 1), ladder)
        for dr in range(2):
            send(ref, ref, ("a0", dr, 1), zdev[dr])

    def lad_a():
        for u in range(2):
            recv(aref(lbrow(z, u)), ("la", u))
        ref = aref(arow(z, 1))
        for dr in range(2):
            send(ref, ref, ("a", dr, 1, 1), zdev[dr])

    def lad_b():
        for u in range(2):
            recv(bref(lbrow(z, u)), ("lb", 0, u, 0))
        own_w.wait()

    def x_cross(c):
        ref = xx.at[NC + c, t]
        recv(ref, ("xc", c))
        for dr in range(2):
            send(ref, ref, ("y", dr, c), ydev[dr])
        send(ref, ref, ("sw", 0, c), other)

    def slice_at(o):
        return (t + 2 * o + NT) % NT

    def x_hop(c, dr):
        ref = xx.at[NC + c, slice_at(-1 if dr == 0 else 1)]
        recv(ref, ("y", dr, c))
        send(ref, ref, ("sw", 1 + dr, c), other)
        if c not in EXTRA and c % 2 == dr:
            send(ref, ref, ("y2", c), ydev[dr])

    def x_far(c):
        ref = xx.at[NC + c, slice_at(2)]
        recv(ref, ("y2", c))
        send(ref, ref, ("sw", 3, c), other)

    def x_swap(c):
        to = 1 - 2 * core
        for k, o in enumerate((0, -1, 1, 2)):
            recv(xx.at[NC + c, (t + to + 2 * o + NT) % NT], ("sw", k, c))

    def mix(m0, half):
        rows = 2 * CH
        for k in range(0, NT, 2):
            a = jnp.concatenate([xx[m0:m0 + 2, k].reshape(rows, KS), xx[m0:m0 + 2, k + 1].reshape(rows, KS)], axis=1)
            p = dot(a, lown[half, k:k + 2].reshape(2 * KS, NM))
            total = p if k == 0 else total + p
        return total.astype(BF)

    def add_output(m0, mixed):
        acc[m0:m0 + 2] -= dot(mixed, rexp[...]).reshape(2, CH, HC)

    def first_mix(m0):
        mixed = mix(m0, 0)
        fm[m0:m0 + 2] = mixed.reshape(2, CH, NM)
        add_output(m0, mixed)

    def partner_mix(p):
        fmo[2 * p:2 * p + 2] = mix(2 * p, 1).reshape(2, CH, NM)
        send(fmo.at[2 * p:2 * p + 2], fm.at[NC + 2 * p:NC + 2 * p + 2], ("fm", p), partner)

    def partner_mix_wait(p):
        recv(fm.at[NC + 2 * p:NC + 2 * p + 2], ("fm", p))

    def partner_output(p):
        add_output(NC + 2 * p, fm[NC + 2 * p:NC + 2 * p + 2].reshape(2 * CH, NM))

    def targets(m0, mc, r_lo, r_n):
        def part(r, carry):
            zv = (z + ((r + 1) // 2) * (2 * (r % 2) - 1) + NZ) % NZ
            a = xx[m0:m0 + mc, zv].reshape(mc * CH, KS)
            w = wb[pl.ds(pl.multiple_of(zv * KS, KS), KS), :]
            p = dot(a, w).reshape(mc, CH, HC)
            if r_lo == 0:
                acc[m0:m0 + mc] = p
            else:
                acc[m0:m0 + mc] += p
            return carry
        lax.fori_loop(r_lo, r_lo + r_n, part, 0)

    col_block = iota((NB, HC), 1) // SO

    def expand_right():
        for c in xloads:
            c.wait()
        for j in range(JB):
            rexp[j * NB:(j + 1) * NB] = jnp.where(col_block == j, rh[...], 0).astype(BF)
        pick = (iota((NM, NB), 0) // JB == iota((NM, NB), 1)).astype(BF)
        spread = dot(pick, rh[...])
        rexp2[...] = jnp.where(iota((NM, HC), 0) % JB == iota((NM, HC), 1) // SO, spread, 0.0).astype(BF)

    def gather_left():
        for k in range(1, NT):
            recv(lall.at[(t + NT - k) % NT], ("l", k))
        lall[t] = lpack[t]

    def expand_left():
        def expand(n, carry):
            half, il = n // 8, n % 8
            want = JB * (side + half * (1 - 2 * side))
            row, col = iota((BK, NM), 0), iota((BK, NM), 1)
            choose = jnp.where((row // 8 == il) & (row % 8 == want + col // NB), 1.0, 0.0).astype(BF)
            p = dot(lall[...].reshape(KS, BK), choose)
            row, col = iota((KS, NM), 0), iota((KS, NM), 1)
            keep = col % NB == (row // NB) * 8 + il
            lown[half, :, il] = jnp.where(keep, p, 0.0).astype(BF).reshape(NT, SI, NM)
            return carry
        lax.fori_loop(0, 16, expand, 0)

    events = {"injb": inj_b, "inja": inj_a, "la": lad_a, "lb0": lad_b, "l": gather_left,
              "rex": expand_right, "exp": expand_left}
    at = 0
    while at < len(ORDER):
        name = ORDER[at]
        at += 1
        nums = [int(ch) for ch in name if ch.isdigit()]
        kind = name.rstrip("0123456789")
        if name in events:
            events[name]()
        elif kind == "f":
            first_mix(2 * nums[0])
        elif kind == "t":
            partner_mix(*nums)
        elif kind == "m":
            partner_mix_wait(*nums)
        elif kind == "g":
            partner_output(*nums)
        elif kind in ("o", "x") and name[0:2] != "x2" or kind == "x" and len(nums) == 2:
            r, n = nums[-1], 1
            while r and at < len(ORDER) and ORDER[at] == name[:-1] + str(r + n):
                n, at = n + 1, at + 1
            if kind == "x" and n == 1 and r and at < len(ORDER) and ORDER[at] == "x1" + str(r) and not nums[0]:
                at += 1
                targets(NC, 4, r, 1)
            else:
                targets(0 if kind == "o" else NC + 2 * nums[0], 4 if kind == "o" else 2, r, n)
        elif kind == "b":
            b_step(*nums)
        elif kind == "lb":
            lb_wait(*nums)
        elif kind == "a":
            a_step(*nums)
        elif kind == "xc":
            x_cross(*nums)
        elif kind == "y":
            x_hop(*nums)
        elif kind == "e":
            x_far(*nums)
        elif kind == "sw":
            x_swap(*nums)
        else:
            raise ValueError(name)

    gr[...] = jnp.zeros_like(gr)
    lossv[...] = jnp.zeros_like(lossv)

    def right_part(p, carry):
        m0 = 2 * p
        a = acc[pl.ds(m0, 2)].reshape(2 * CH, HC)
        lossv[...] += jnp.sum((a * a).reshape(2 * CH // 8, 8, HC), axis=0)
        sl = (a * (-1.0 / TOKENS)).astype(BF)
        slope[p] = sl
        gr[...] += lax.dot_general(fm[pl.ds(m0, 2)].reshape(2 * CH, NM), sl, TN_DIMS, preferred_element_type=F32)
        return carry
    lax.fori_loop(0, 4, right_part, 0)
    right = jnp.zeros((NB, HC), F32)
    for j in range(JB):
        right += jnp.where(col_block == j, gr[j * NB:(j + 1) * NB], 0.0)
    ggr[...] = right
    s8r[:, HC:RW] = jnp.full((8, 128), jnp.sum(lossv[...]), F32)

    def rows_of(zv):
        return pl.ds(pl.multiple_of(zv * 8, 8), 8)

    def z_send(src, dst, key):
        for k in (4, 3, 5, 2, 6, 1, 7):
            send(src.at[rows_of((z + k) % NZ)], dst.at[k], (key, k), dp_dev(x, (z + k) % NZ))

    def z_sum(src, dst, key, out):
        total = src[rows_of(z), :]
        for k in range(1, NZ):
            recv(dst.at[k], (key, k))
            total += dst[k]
        out[:, 0:total.shape[1]] = total
        return total

    z_send(ggr, zrr, "zr")

    def back_part(p, carry):
        bmt[p] = lax.dot_general(rexp2[...], slope[p], NT_DIMS, preferred_element_type=F32).astype(BF)
        return carry
    lax.fori_loop(0, 4, back_part, 0)

    def left_part(k, carry):
        rows = pl.ds(pl.multiple_of(k * 32, 32), 32)
        total = dot(bmt[0, rows, :], xx[0:2, k].reshape(2 * CH, KS))
        for p in range(1, 4):
            total += dot(bmt[p, rows, :], xx[2 * p:2 * p + 2, k].reshape(2 * CH, KS))
        gl[k] = total
        return carry
    lax.fori_loop(0, NT, left_part, 0)
    row32 = iota((32, 128), 0)
    folded = []
    for k in range(NT):
        v = jnp.zeros((32, 128), F32)
        for p in range(4):
            v += jnp.where(row32 // 8 == p, gl[k, :, p * 128:(p + 1) * 128], 0.0)
        folded.append(jnp.where((row32 // 4) % 2 == 0, v, pltpu.roll(v, 64, 1)))
    ggl[...] = jnp.transpose(jnp.concatenate(folded, axis=0))[0:SI]
    z_send(ggl, zrl, "zl")

    total_r = z_sum(ggr, zrr, "zr", s8r)
    send(s8r, xrr, ("xr",), ladder)
    total_l = z_sum(ggl, zrl, "zl", s8l)
    send(s8l, xrl, ("xl",), ladder)
    recv(xrr, ("xr",))
    full_r = total_r + xrr[:, 0:HC]
    loss_part = s8r[:, HC:RW] + xrr[:, HC:RW]
    sq_right = jnp.sum(full_r * full_r)
    recv(xrl, ("xl",))
    full_l = total_l + xrl[...]
    sq_left = jnp.sum(full_l * full_l)
    srow = iota((8, 128), 0)
    tot = jnp.where(srow == 0, sq_right, jnp.where(srow == 1, sq_left, jnp.where(srow == 2, loss_part, 0.0)))
    sc[...] = tot
    for k in (4, 3, 5, 2, 6, 1, 7, 0):
        if k:
            send(sc, scz.at[k], ("sz", k), dp_dev(x, (z + k) % NZ))
        send(sc, scz.at[NZ + k], ("sz", NZ + k), dp_dev(px, (z + k) % NZ))
    s8f[:, 0:HC] = full_r
    s8f[:, HC:HC + NM] = full_l
    send(s8f, xrf, ("xf",), partner)

    def own(v):
        out = v[0:2]
        for k in range(1, NX):
            out = jnp.where(x == k, v[2 * k:2 * k + 2], out)
        return out

    recv(xrf, ("xf",))
    mine, theirs = own(s8f[...]), own(xrf[...])
    rows_a = jnp.where(side == 0, mine, theirs)
    rows_b = jnp.where(side == 0, theirs, mine)
    glr[t] = jnp.zeros((8, 2 * NM), F32)
    glr[t, 0:2, 0:NM] = rows_a[:, HC:HC + NM]
    glr[t, 0:2, NM:2 * NM] = rows_b[:, HC:HC + NM]
    for k in range(1, NT):
        send(glr.at[t], glr.at[t], ("gl", k), t_dev((t + k) % NT))
    for k in range(1, 2 * NZ):
        recv(scz.at[k], ("sz", k))
        tot += scz[k]
    sct[0] = tot
    for k in range(1, NT):
        send(sct.at[0], sct.at[k], ("st", k), t_dev((t + k) % NT))
    lane, col = iota((NM, KS), 0), iota((NM, KS), 1)
    place = jnp.where((lane // JB == 8 * t + col // NB) & (lane % JB == col % JB), 1.0, 0.0)
    for k in range(1, NT):
        recv(glr.at[(t + NT - k) % NT], ("gl", k))
    parts = [glr[k, :, h * NM:(h + 1) * NM] for k in range(NT) for h in range(2)]
    moved = jnp.dot(jnp.concatenate(parts, axis=0), place, precision=lax.Precision.HIGHEST,
                    preferred_element_type=F32)
    mrow, mcol = iota((128, KS), 0), iota((128, KS), 1)
    moved = jnp.where(mrow // 8 == (mcol % NB) // JB, moved, 0.0)
    left_rows = jnp.sum(moved.reshape(16, 8, KS), axis=0)[0:2]
    for k in range(1, NT):
        recv(sct.at[k], ("st", k))
        tot += sct[k]
    scale_right = lax.rsqrt(tot[0:1, 0:1] / (NB * F) + EPS)
    scale_left = lax.rsqrt(tot[1:2, 0:1] / (SI * MID) + EPS)
    dr_out[:, 0:HC] = rows_a[:, 0:HC] * scale_right
    dr_out[:, HC:2 * HC] = rows_b[:, 0:HC] * scale_right
    dl_out[...] = left_rows * scale_left
    loss_out[...] = tot[2:3, :] / (2.0 * TOKENS)
    for copy in sends:
        copy.wait_send()


def local(tokens, dense_weight, left_factor, right_factor):
    vmem = pl.BlockSpec(memory_space=pltpu.VMEM)
    hbm = pl.BlockSpec(memory_space=pl.ANY)
    dir_left, dir_right, loss = pl.pallas_call(
        kernel,
        out_shape=(jax.ShapeDtypeStruct((2, KS), F32),
                   jax.ShapeDtypeStruct((2, 2 * HC), F32),
                   jax.ShapeDtypeStruct((1, 128), F32)),
        in_specs=[hbm] * 4,
        out_specs=(vmem,) * 3,
        scratch_shapes=[
            pltpu.VMEM((2 * NC, NT, CH, KS), BF),
            pltpu.VMEM((4096, HC), BF),
            pltpu.VMEM((SI, KS), BF),
            pltpu.VMEM((NT, SI, BK), BF),
            pltpu.VMEM((NT, SI, BK), BF),
            pltpu.VMEM((2, NT, 8, SI, NM), BF),
            pltpu.VMEM((NB, HC), BF),
            pltpu.VMEM((NM, HC), BF),
            pltpu.VMEM((NM, HC), BF),
            pltpu.VMEM((2 * NC, CH, NM), BF),
            pltpu.VMEM((NC, CH, NM), BF),
            pltpu.VMEM((2 * NC, CH, HC), F32),
            pltpu.VMEM((NC, 2 * CH, HC), BF),
            pltpu.VMEM((NC, NM, 2 * CH), BF),
            pltpu.VMEM((NM, HC), F32),
            pltpu.VMEM((NT, 32, KS), F32),
            pltpu.VMEM((8, HC), F32),
            pltpu.VMEM((NB, HC), F32),
            pltpu.VMEM((NB, NM), F32),
            pltpu.VMEM((NZ, 8, HC), F32),
            pltpu.VMEM((NZ, 8, NM), F32),
            pltpu.VMEM((8, RW), F32),
            pltpu.VMEM((8, NM), F32),
            pltpu.VMEM((8, RW), F32),
            pltpu.VMEM((8, NM), F32),
            pltpu.VMEM((8, HC + NM), F32),
            pltpu.VMEM((8, HC + NM), F32),
            pltpu.VMEM((8, 128), F32),
            pltpu.VMEM((2 * NZ, 8, 128), F32),
            pltpu.VMEM((NT, 8, 128), F32),
            pltpu.VMEM((NT, 8, 2 * NM), F32),
            pltpu.SemaphoreType.DMA((176,)),
            pltpu.SemaphoreType.DMA((176,)),
            pltpu.SemaphoreType.DMA((16,)),
        ],
        compiler_params=pltpu.CompilerParams(
            collective_id=0, has_side_effects=True, vmem_limit_bytes=60 * 1024 * 1024),
    )(tokens.reshape(NC, CH, 4096), dense_weight, left_factor, right_factor)
    return (dir_left, dir_right, loss[0, 0])


def solution(mesh):
    in_specs = (P("dp", None), P("dp", "tensor"), P(None, "tensor"), P(None, "tensor"))
    out_specs = (P("dp", "tensor"), P("dp", "tensor"), P())
    return jax.shard_map(local, mesh=mesh, in_specs=in_specs, out_specs=out_specs, check_vma=False)
```
